32 devices in a mesh: section: 2 (over x), mirror: 2 (over y), dp: 8 (over z, core).
Axes of the slice: x: 2, y: 2, z: 4, core: 2. Of those that a mesh axis runs over, the one named last changes fastest.
Arguments:
- sent_fwd: bfloat16 [2, 2, 8, 4096], P('section', 'mirror', 'dp'), may hold values from -36 to 36
- sent_bwd: bfloat16 [2, 2, 8, 4096], P('section', 'mirror', 'dp'), may hold values from -6 to 6
- stash: bfloat16 [2, 2, 8, 4096], P('section', 'mirror', 'dp'), may hold values from -36 to 36
- gain: float32 [2, 4096], P('section'), may hold values from 0.5 to 1.5
- w_in: bfloat16 [2, 4096, 1024], P('section', None, 'dp'), may hold values from -0.09375 to 0.09375
- w_out: bfloat16 [2, 1024, 4096], P('section', 'dp'), may hold values from -0.375 to 0.375
Outputs:
- fwd_out: bfloat16 [2, 2, 8, 4096], P('section', 'mirror', 'dp')
- bwd_out: bfloat16 [2, 2, 8, 4096], P('section', 'mirror', 'dp')
- w_in_grad: bfloat16 [2, 4096, 1024], P('section', 'mirror', 'dp')
- w_out_grad: bfloat16 [2, 1024, 4096], P('section', 'dp', 'mirror')
The draws below stay inside these ranges and needn't reach their ends.
All inputs are finite; a program needn't handle non-finite values.
Results may differ from the reference program's by a relative error of at most 0.0068.
Values may be sent and summed in bfloat16 or wider, within the bound.
No kernel may reach another device: no remote copies, remote signals or barrier semaphores. Data moves between devices by JAX's collectives and lax.ppermute only.
A program may use at most 64 MiB of HBM per device.

```python
import math
import jax
import jax.numpy as jnp
from jax import lax

D = 4096
ROWS = 8
FF = 1024
N_SECTION = 2


def scaled_acts(key):
    keys = jax.random.split(key, 3)
    shape = (N_SECTION, 2, ROWS, D)
    base = jnp.clip(jax.random.normal(keys[0], shape, jnp.float32), -4.0, 4.0)
    column = jnp.exp(jax.random.uniform(keys[1], (D,), jnp.float32, math.log(0.3), math.log(3.0)))
    row_scale = jnp.exp(jax.random.uniform(keys[2], (N_SECTION, 2, ROWS, 1), jnp.float32, math.log(0.3), math.log(3.0)))
    return (base * column * row_scale).astype(jnp.bfloat16)


def draw_sent_fwd(key, part):
    return scaled_acts(jax.random.fold_in(key, 11))


def draw_stash(key, part):
    return scaled_acts(jax.random.fold_in(key, 23))


def level_of(rng, extent, cuts, smallest, top_value):
    level = 1.0
    for axis_at, blocks in cuts:
        heights = jax.random.uniform(jax.random.fold_in(jax.random.fold_in(rng, 6), axis_at), (blocks,), jnp.float32, smallest / len(cuts), top_value / len(cuts))
        level = level * jnp.repeat(jnp.exp(heights), extent[axis_at] // blocks).reshape((-1,) + (1,) * (len(extent) - 1 - axis_at))
    return level


def noise(rng, extent, scale, bound, pieces=(), kind=jnp.bfloat16):
    entries = scale * jax.random.normal(rng, extent, jnp.float32)
    if pieces:
        entries = entries * level_of(rng, extent, pieces, -0.22, 0.18)
    return jnp.clip(entries, -bound, bound).astype(kind)


def setup_inputs(seed: int = 0) -> dict:
    seeds = jax.random.split(jax.random.key(seed), 7)
    return {
        "sent_fwd": draw_sent_fwd(jax.random.fold_in(seeds[6], 71), 0),
        "sent_bwd": noise(seeds[1], (N_SECTION, 2, ROWS, D), 1.0, 6.0, ((0, 2), (1, 2), (2, 8))),
        "stash": draw_stash(jax.random.fold_in(seeds[6], 71), 0),
        "gain": jnp.clip(1.0 + 0.1 * jax.random.normal(seeds[3], (N_SECTION, D), jnp.float32), 0.5, 1.5),
        "w_in": noise(seeds[4], (N_SECTION, D, FF), D ** -0.5, 0.09375, ((0, 2), (2, 8))),
        "w_out": noise(seeds[5], (N_SECTION, FF, D), (FF // 4) ** -0.5, 0.375, ((0, 2), (1, 8))),
    }


def norm_rows(x):
    centre = x - lax.optimization_barrier(jnp.mean(x, axis=-1, keepdims=True))
    rstd = lax.rsqrt(lax.optimization_barrier(jnp.mean(centre * centre, axis=-1, keepdims=True)) + 1e-05)
    return (centre * rstd, rstd)

def gelu_pair(h):
    coeff = 0.7978845608028654
    inner = coeff * (h + 0.044715 * h * h * h)
    tanh_val = jnp.tanh(inner)
    value = 0.5 * h * (1.0 + tanh_val)
    slope = 0.5 * (1.0 + tanh_val) + 0.5 * h * (1.0 - tanh_val * tanh_val) * coeff * (1.0 + 3.0 * 0.044715 * h * h)
    return (value, slope)

def block_forward(x, gain_row, w_first, w_second):
    x_full = x.astype(jnp.float32)
    nhat, _ = norm_rows(x_full)
    normed = (nhat * gain_row).astype(jnp.bfloat16)
    hidden = jnp.dot(normed, w_first, preferred_element_type=jnp.float32)
    acted = gelu_pair(hidden)[0].astype(jnp.bfloat16)
    return (x_full + jnp.dot(acted, w_second, preferred_element_type=jnp.float32)).astype(jnp.bfloat16)

def block_backward(x, cotan, gain_row, w_first, w_second):
    nhat, rstd = norm_rows(x.astype(jnp.float32))
    normed = (nhat * gain_row).astype(jnp.bfloat16)
    hidden = jnp.dot(normed, w_first, preferred_element_type=jnp.float32)
    value, slope = gelu_pair(hidden)
    acted = value.astype(jnp.bfloat16)
    grad_second = jnp.dot(acted.T, cotan, preferred_element_type=jnp.float32)
    d_acted = jnp.dot(cotan, w_second.T, preferred_element_type=jnp.float32)
    d_hidden = (d_acted * slope).astype(jnp.bfloat16)
    grad_first = jnp.dot(normed.T, d_hidden, preferred_element_type=jnp.float32)
    d_normed = jnp.dot(d_hidden, w_first.T, preferred_element_type=jnp.float32)
    scaled = d_normed * gain_row
    d_input = rstd * (scaled - lax.optimization_barrier(jnp.mean(scaled, axis=-1, keepdims=True)) - nhat * lax.optimization_barrier(jnp.mean(scaled * nhat, axis=-1, keepdims=True)))
    return ((cotan.astype(jnp.float32) + d_input).astype(jnp.bfloat16), grad_first, grad_second)

def rounded(values):
    return lax.optimization_barrier(values.astype(jnp.bfloat16)).astype(jnp.float32)

def reference(sent_fwd, sent_bwd, stash, gain, w_in, w_out):
    sections = N_SECTION
    forward_list = []
    backward_list = []
    first_grads = []
    second_grads = []
    for section_pos in range(sections):
        fwd_row = []
        bwd_row = []
        total_first = jnp.zeros(w_in.shape[1:], jnp.float32)
        total_second = jnp.zeros(w_out.shape[1:], jnp.float32)
        for pipe in range(2):
            if pipe == 0:
                src_fwd = (section_pos - 1) % sections
                src_bwd = (section_pos + 1) % sections
            else:
                src_fwd = (section_pos + 1) % sections
                src_bwd = (section_pos - 1) % sections
            fwd_row.append(block_forward(sent_fwd[src_fwd, pipe], gain[section_pos], w_in[section_pos], w_out[section_pos]))
            d_input, grad_first, grad_second = block_backward(stash[section_pos, pipe], sent_bwd[src_bwd, pipe], gain[section_pos], w_in[section_pos], w_out[section_pos])
            bwd_row.append(d_input)
            total_first = total_first + rounded(grad_first)
            total_second = total_second + rounded(grad_second)
        forward_list.append(jnp.stack(fwd_row))
        backward_list.append(jnp.stack(bwd_row))
        first_grads.append(total_first.astype(jnp.bfloat16))
        second_grads.append(total_second.astype(jnp.bfloat16))
    return (jnp.stack(forward_list), jnp.stack(backward_list), jnp.stack(first_grads), jnp.stack(second_grads))
```

```python
import jax
import jax.numpy as jnp
from jax import lax
from jax.sharding import PartitionSpec as P

AXES = ("section", "mirror", "dp")


def xor_pairs(count, mask):
    return [(source, source ^ mask) for source in range(count)]


def relay_pairs(sections, mirrors, count, mask):
    pairs = []
    for section in range(sections):
        for mirror in range(mirrors):
            step = 1 if mirror == 0 else -1
            for dp in range(count):
                source = (section * mirrors + mirror) * count + dp
                target = ((section + step) % sections * mirrors + mirror) * count + (dp ^ mask)
                pairs.append((source, target))
    return pairs


def norm_rows(x):
    centre = x - jnp.mean(x, axis=-1, keepdims=True)
    rstd = lax.rsqrt(jnp.mean(centre * centre, axis=-1, keepdims=True) + 1e-05)
    return (centre * rstd, rstd)


def gelu_pair(h):
    coeff = 0.7978845608028654
    inner = coeff * (h + 0.044715 * h * h * h)
    tanh_val = jnp.tanh(inner)
    value = 0.5 * h * (1.0 + tanh_val)
    slope = 0.5 * (1.0 + tanh_val) + 0.5 * h * (1.0 - tanh_val * tanh_val) * coeff * (
        1.0 + 3.0 * 0.044715 * h * h
    )
    return (value, slope)


def rounded(values):
    return lax.optimization_barrier(values.astype(jnp.bfloat16)).astype(jnp.float32)


def on_device(sent_fwd, sent_bwd, stash, gain, w_in, w_out):
    sections, mirrors = lax.axis_size("section"), lax.axis_size("mirror")
    count = lax.axis_size("dp")
    bits = count.bit_length() - 1
    masks = [(1 << bit) | 1 for bit in range(bits - 1, 0, -1)]
    mirror_pos = lax.axis_index("mirror")
    rows, width = sent_fwd.shape[2], sent_fwd.shape[3]
    gain_row = gain[0]
    w_first = w_in[0]
    w_second = w_out[0]
    fwd_in = lax.ppermute(sent_fwd[0, 0], AXES, relay_pairs(sections, mirrors, count, 1))
    back = [(target ^ 1, source ^ 1) for source, target in relay_pairs(sections, mirrors, count, 1)]
    bwd_in = lax.ppermute(sent_bwd[0, 0], AXES, back)
    held = jnp.stack([fwd_in, bwd_in, stash[0, 0]])
    for mask in masks:
        other = lax.ppermute(held, "dp", xor_pairs(count, mask))
        held = jnp.concatenate([held, other], axis=1)
    other = lax.ppermute(held, "dp", xor_pairs(count, 1))
    whole_fin = jnp.concatenate([other[0], held[0]], axis=0)
    whole_cotan = jnp.concatenate([other[1], held[1]], axis=0)
    whole_stash = jnp.concatenate([held[2], other[2]], axis=0)
    nhat_fwd, _ = norm_rows(whole_fin.astype(jnp.float32))
    whole_fwd = (nhat_fwd * gain_row).astype(jnp.bfloat16)
    nhat_bwd, rstd_bwd = norm_rows(whole_stash.astype(jnp.float32))
    whole_bwd = (nhat_bwd * gain_row).astype(jnp.bfloat16)
    hidden_fwd = jnp.dot(whole_fwd, w_first, preferred_element_type=jnp.float32)
    acted_fwd = gelu_pair(hidden_fwd)[0].astype(jnp.bfloat16)
    hidden_bwd = jnp.dot(whole_bwd, w_first, preferred_element_type=jnp.float32)
    value_bwd, slope_bwd = gelu_pair(hidden_bwd)
    acted_bwd = value_bwd.astype(jnp.bfloat16)
    d_acted = jnp.dot(whole_cotan, w_second.T, preferred_element_type=jnp.float32)
    d_hidden = (d_acted * slope_bwd).astype(jnp.bfloat16)
    part_fwd = jnp.dot(acted_fwd, w_second, preferred_element_type=jnp.float32)
    part_bwd = jnp.dot(d_hidden, w_first.T, preferred_element_type=jnp.float32)
    part = jnp.stack([part_fwd, part_bwd])
    for mask in [1] + masks[::-1]:
        half = part.shape[1] // 2
        sent = part[:, half:].astype(jnp.bfloat16)
        came = lax.ppermute(sent, "dp", xor_pairs(count, mask))
        part = part[:, :half] + came.astype(jnp.float32)
    branch_sum, d_normed = part[0], part[1]
    fwd_result = (whole_fin[:rows].astype(jnp.float32) + branch_sum).astype(jnp.bfloat16)
    scaled = d_normed * gain_row
    nhat_own = nhat_bwd[:rows]
    d_input = rstd_bwd[:rows] * (
        scaled
        - jnp.mean(scaled, axis=-1, keepdims=True)
        - nhat_own * jnp.mean(scaled * nhat_own, axis=-1, keepdims=True)
    )
    bwd_result = (whole_cotan[:rows].astype(jnp.float32) + d_input).astype(jnp.bfloat16)
    half_width = width // 2
    own_start = mirror_pos * half_width
    other_start = (1 - mirror_pos) * half_width

    def columns(value, start):
        return lax.dynamic_slice_in_dim(value, start, half_width, 1)

    outgoing = jnp.concatenate(
        [columns(whole_bwd, other_start), columns(whole_cotan, other_start), acted_bwd, d_hidden], axis=1
    )
    far = lax.ppermute(outgoing, "mirror", xor_pairs(mirrors, 1))
    far_bwd, far_cotan = far[:, :half_width], far[:, half_width : 2 * half_width]
    far_acted, far_hidden = jnp.split(far[:, 2 * half_width :], 2, axis=1)

    def outer(left, right):
        return jnp.dot(left.T, right, preferred_element_type=jnp.float32)

    summed_first = rounded(outer(columns(whole_bwd, own_start), d_hidden)) + rounded(outer(far_bwd, far_hidden))
    summed_second = rounded(outer(acted_bwd, columns(whole_cotan, own_start))) + rounded(outer(far_acted, far_cotan))
    return (
        fwd_result[None, None],
        bwd_result[None, None],
        summed_first.astype(jnp.bfloat16)[None],
        summed_second.astype(jnp.bfloat16)[None],
    )


def solution(mesh):
    in_specs = (
        P("section", "mirror", "dp", None),
        P("section", "mirror", "dp", None),
        P("section", "mirror", "dp", None),
        P("section", None),
        P("section", None, "dp"),
        P("section", "dp", None),
    )
    out_specs = (
        P("section", "mirror", "dp", None),
        P("section", "mirror", "dp", None),
        P("section", "mirror", "dp"),
        P("section", "dp", "mirror"),
    )
    return jax.shard_map(
        on_device, mesh=mesh, in_specs=in_specs, out_specs=out_specs, check_vma=False
    )
```

```python
import functools

import jax
import jax.numpy as jnp
from jax import lax
from jax.experimental import pallas as pl
from jax.experimental.pallas import tpu as pltpu
from jax.sharding import PartitionSpec as P

AXES = ("section", "mirror", "dp")
VMEM = pl.BlockSpec(memory_space=pltpu.VMEM)


def xor_pairs(count, mask):
    return [(source, source ^ mask) for source in range(count)]


def relay_pairs(sections, mirrors, count, mask, sign):
    pairs = []
    for section in range(sections):
        for mirror in range(mirrors):
            step = sign if mirror == 0 else -sign
            for dp in range(count):
                source = (section * mirrors + mirror) * count + dp
                target = ((section + step) % sections * mirrors + mirror) * count + (dp ^ mask)
                pairs.append((source, target))
    return sorted(pairs)


def norm_rows(x):
    centre = x - jnp.mean(x, axis=-1, keepdims=True)
    rstd = lax.rsqrt(jnp.mean(centre * centre, axis=-1, keepdims=True) + 1e-05)
    return (centre * rstd, rstd)


def gelu_pair(h):
    coeff = 0.7978845608028654
    inner = coeff * (h + 0.044715 * h * h * h)
    tanh_val = jnp.tanh(inner)
    value = 0.5 * h * (1.0 + tanh_val)
    slope = 0.5 * (1.0 + tanh_val) + 0.5 * h * (1.0 - tanh_val * tanh_val) * coeff * (
        1.0 + 3.0 * 0.044715 * h * h
    )
    return (value, slope)


def dot(left, right, contract):
    return lax.dot_general(left, right, ((contract[:1], contract[1:]), ((), ())), preferred_element_type=jnp.float32)


def block_kernel(rows, held, other, gain, w_in, w_out, send, keep, own_out, far_out, tail, tail_rstd):
    half, width = held.shape[1], held.shape[2]
    f32, bf16 = jnp.float32, jnp.bfloat16

    def joined(first, second):
        return jnp.concatenate([first.astype(f32), second.astype(f32)], axis=0)

    fin = joined(other[0], held[0])
    cotan = joined(other[1], held[1])
    stash = joined(held[2], other[2])
    nhat_fwd, _ = norm_rows(fin)
    nhat_bwd, rstd_bwd = norm_rows(stash)
    normed_bwd = nhat_bwd * gain[...]
    both = jnp.concatenate([nhat_fwd * gain[...], normed_bwd], axis=0).astype(bf16)
    hidden = dot(both, w_in[...], (1, 0))
    cotan_low = cotan.astype(bf16)
    d_acted = dot(cotan_low, w_out[...], (1, 1))
    value, slope = gelu_pair(hidden)
    value_low = value.astype(bf16)
    d_hidden = (d_acted * slope[2 * half :]).astype(bf16)
    part_bwd = dot(d_hidden, w_in[...], (1, 1))
    part_fwd = dot(value_low[: 2 * half], w_out[...], (1, 0))
    keep[0] = part_fwd[:half]
    keep[1] = part_bwd[:half]
    send[0] = part_fwd[half:].astype(bf16)
    send[1] = part_bwd[half:].astype(bf16)
    tail[0] = fin[:rows]
    tail[1] = cotan[:rows]
    tail[2] = nhat_bwd[:rows]
    tail_rstd[...] = jnp.broadcast_to(rstd_bwd[:rows], tail_rstd.shape)
    mid = width // 2
    units = w_in.shape[1]
    normed_low = normed_bwd.astype(bf16)
    upper = lax.axis_index("mirror") == 0
    for ref in (own_out, far_out):
        ref[:, 2 * mid : 2 * mid + units] = value_low[2 * half :]
        ref[:, 2 * mid + units :] = d_hidden

    @pl.when(upper)
    def _():
        own_out[:, :mid] = normed_low[:, :mid]
        own_out[:, mid : 2 * mid] = cotan_low[:, :mid]
        far_out[:, :mid] = normed_low[:, mid:]
        far_out[:, mid : 2 * mid] = cotan_low[:, mid:]

    @pl.when(jnp.logical_not(upper))
    def _():
        own_out[:, :mid] = normed_low[:, mid:]
        own_out[:, mid : 2 * mid] = cotan_low[:, mid:]
        far_out[:, :mid] = normed_low[:, :mid]
        far_out[:, mid : 2 * mid] = cotan_low[:, :mid]


def load_kernel(chunks, source, target, sems):
    step = source.shape[0] // chunks
    copies = [
        pltpu.make_async_copy(source.at[pl.ds(i * step, step)], target.at[pl.ds(i * step, step)], sems.at[i])
        for i in range(chunks)
    ]
    for copy in copies:
        copy.start()
    for copy in copies:
        copy.wait()


def loaded(weights, chunks):
    size = weights.size * weights.dtype.itemsize
    return pl.pallas_call(
        functools.partial(load_kernel, chunks),
        out_shape=jax.ShapeDtypeStruct(weights.shape, weights.dtype),
        in_specs=[pl.BlockSpec(memory_space=pl.ANY)],
        out_specs=VMEM,
        scratch_shapes=[pltpu.SemaphoreType.DMA((chunks,))],
        compiler_params=pltpu.CompilerParams(vmem_limit_bytes=max(4 << 20, 2 * size)),
        cost_estimate=pl.CostEstimate(flops=0, bytes_accessed=3 * size, transcendentals=0),
    )(weights)


def tail_kernel(rows, part, came, gain, tail, tail_rstd, fwd_out, bwd_out):
    f32 = jnp.float32
    branch = part[0, :rows] + came[0].astype(f32)
    fwd_out[...] = (tail[0] + branch).astype(fwd_out.dtype)
    scaled = (part[1, :rows] + came[1].astype(f32)) * gain[...]
    nhat = tail[2]
    d_input = tail_rstd[:, :1] * (
        scaled
        - jnp.mean(scaled, axis=-1, keepdims=True)
        - nhat * jnp.mean(scaled * nhat, axis=-1, keepdims=True)
    )
    bwd_out[...] = (tail[1] + d_input).astype(bwd_out.dtype)


def on_device(sent_fwd, sent_bwd, stash, gain, w_in, w_out):
    sections, mirrors = lax.axis_size("section"), lax.axis_size("mirror")
    count = lax.axis_size("dp")
    bits = count.bit_length() - 1
    masks = [(1 << bit) | 1 for bit in range(bits - 1, 0, -1)]
    rows, width = sent_fwd.shape[2], sent_fwd.shape[3]
    units = w_in.shape[2]
    fwd_in = lax.ppermute(sent_fwd[0, 0], AXES, relay_pairs(sections, mirrors, count, 1, 1))
    bwd_in = lax.ppermute(sent_bwd[0, 0], AXES, relay_pairs(sections, mirrors, count, 1, -1))
    w_first = loaded(w_in[0], 4)
    fwd_in, bwd_in, w_first = lax.optimization_barrier((fwd_in, bwd_in, w_first))
    w_second = loaded(w_out[0], 4)
    held = jnp.stack([fwd_in, bwd_in, stash[0, 0]])
    for mask in masks:
        other = lax.ppermute(held, "dp", xor_pairs(count, mask))
        if mask == masks[0]:
            other, w_second = lax.optimization_barrier((other, w_second))
        held = jnp.concatenate([held, other], axis=1)
    other = lax.ppermute(held, "dp", xor_pairs(count, 1))
    half = held.shape[1]
    low = jax.ShapeDtypeStruct((2 * half, width + 2 * units), jnp.bfloat16)
    send, keep, own, away, tail, tail_rstd = pl.pallas_call(
        functools.partial(block_kernel, rows),
        out_shape=(
            jax.ShapeDtypeStruct((2, half, width), jnp.bfloat16),
            jax.ShapeDtypeStruct((2, half, width), jnp.float32),
            low,
            low,
            jax.ShapeDtypeStruct((3, rows, width), jnp.float32),
            jax.ShapeDtypeStruct((rows, 128), jnp.float32),
        ),
        in_specs=[VMEM] * 5,
        out_specs=[VMEM] * 6,
        compiler_params=pltpu.CompilerParams(vmem_limit_bytes=max(8 << 20, 40 * half * width * 4)),
    )(held, other, gain, w_first, w_second)
    part = None
    for mask in [1] + masks[::-1]:
        if part is not None:
            half = part.shape[1] // 2
            send, keep = part[:, half:].astype(jnp.bfloat16), part[:, :half]
        came = lax.ppermute(send, "dp", xor_pairs(count, mask))
        if mask != (masks or [1])[0]:
            part = keep + came.astype(jnp.float32)
            if mask == 1:
                part, away = lax.optimization_barrier((part, away))
    far = lax.ppermute(away, "mirror", xor_pairs(mirrors, 1))
    pair = jnp.concatenate([own, far], axis=0)
    mid = width // 2
    grad_first = dot(pair[:, :mid], pair[:, 2 * mid + units :], (0, 0)).astype(jnp.bfloat16)
    grad_second = dot(pair[:, 2 * mid : 2 * mid + units], pair[:, mid : 2 * mid], (0, 0)).astype(jnp.bfloat16)
    part, grad_first, grad_second = lax.optimization_barrier((part, grad_first, grad_second))
    fwd_out, bwd_out = pl.pallas_call(
        functools.partial(tail_kernel, rows),
        out_shape=(jax.ShapeDtypeStruct((rows, width), jnp.bfloat16),) * 2,
        in_specs=[VMEM] * 5,
        out_specs=[VMEM] * 2,
        compiler_params=pltpu.CompilerParams(vmem_limit_bytes=max(4 << 20, 40 * rows * width * 4)),
    )(part, came, gain, tail, tail_rstd)
    return (fwd_out[None, None], bwd_out[None, None], grad_first[None], grad_second[None])


def solution(mesh):
    in_specs = (
        P("section", "mirror", "dp", None),
        P("section", "mirror", "dp", None),
        P("section", "mirror", "dp", None),
        P("section", None),
        P("section", None, "dp"),
        P("section", "dp", None),
    )
    out_specs = (
        P("section", "mirror", "dp", None),
        P("section", "mirror", "dp", None),
        P("section", "mirror", "dp"),
        P("section", "dp", "mirror"),
    )
    return jax.shard_map(
        on_device, mesh=mesh, in_specs=in_specs, out_specs=out_specs, check_vma=False
    )
```

```python
import functools

import jax
import jax.numpy as jnp
from jax import lax
from jax.experimental import pallas as pl
from jax.experimental.pallas import tpu as pltpu
from jax.sharding import PartitionSpec as P

AXES = ("section", "mirror", "dp")
VMEM = pl.BlockSpec(memory_space=pltpu.VMEM)


def xor_pairs(count, mask):
    return [(source, source ^ mask) for source in range(count)]


def relay_pairs(sections, mirrors, count, mask, sign):
    pairs = []
    for section in range(sections):
        for mirror in range(mirrors):
            step = sign if mirror == 0 else -sign
            for dp in range(count):
                source = (section * mirrors + mirror) * count + dp
                target = ((section + step) % sections * mirrors + mirror) * count + (dp ^ mask)
                pairs.append((source, target))
    return sorted(pairs)


def norm_rows(x):
    centre = x - jnp.mean(x, axis=-1, keepdims=True)
    rstd = lax.rsqrt(jnp.mean(centre * centre, axis=-1, keepdims=True) + 1e-05)
    return (centre * rstd, rstd)


def gelu_pair(h):
    coeff = 0.7978845608028654
    inner = coeff * (h + 0.044715 * h * h * h)
    tanh_val = jnp.tanh(inner)
    value = 0.5 * h * (1.0 + tanh_val)
    slope = 0.5 * (1.0 + tanh_val) + 0.5 * h * (1.0 - tanh_val * tanh_val) * coeff * (
        1.0 + 3.0 * 0.044715 * h * h
    )
    return (value, slope)


def dot(left, right, contract):
    return lax.dot_general(left, right, ((contract[:1], contract[1:]), ((), ())), preferred_element_type=jnp.float32)


def block_kernel(rows, held, other, gain, w_in, w_out, send, keep, own_out, far_out, tail, tail_rstd):
    half, width = held.shape[1], held.shape[2]
    f32, bf16 = jnp.float32, jnp.bfloat16

    def joined(first, second):
        return jnp.concatenate([first.astype(f32), second.astype(f32)], axis=0)

    fin = joined(other[0], held[0])
    cotan = joined(other[1], held[1])
    stash = joined(held[2], other[2])
    nhat_fwd, _ = norm_rows(fin)
    nhat_bwd, rstd_bwd = norm_rows(stash)
    normed_bwd = nhat_bwd * gain[...]
    both = jnp.concatenate([nhat_fwd * gain[...], normed_bwd], axis=0).astype(bf16)
    hidden = dot(both, w_in[...], (1, 0))
    cotan_low = cotan.astype(bf16)
    d_acted = dot(cotan_low, w_out[...], (1, 1))
    value, slope = gelu_pair(hidden)
    value_low = value.astype(bf16)
    d_hidden = (d_acted * slope[2 * half :]).astype(bf16)
    part_bwd = dot(d_hidden, w_in[...], (1, 1))
    part_fwd = dot(value_low[: 2 * half], w_out[...], (1, 0))
    keep[0] = part_fwd[:half]
    keep[1] = part_bwd[:half]
    send[0] = part_fwd[half:].astype(bf16)
    send[1] = part_bwd[half:].astype(bf16)
    tail[0] = fin[:rows]
    tail[1] = cotan[:rows]
    tail[2] = nhat_bwd[:rows]
    tail_rstd[...] = jnp.broadcast_to(rstd_bwd[:rows], tail_rstd.shape)
    mid = width // 2
    units = w_in.shape[1]
    normed_low = normed_bwd.astype(bf16)
    upper = lax.axis_index("mirror") == 0
    for ref in (own_out, far_out):
        ref[:, 2 * mid : 2 * mid + units] = value_low[2 * half :]
        ref[:, 2 * mid + units :] = d_hidden

    @pl.when(upper)
    def _():
        own_out[:, :mid] = normed_low[:, :mid]
        own_out[:, mid : 2 * mid] = cotan_low[:, :mid]
        far_out[:, :mid] = normed_low[:, mid:]
        far_out[:, mid : 2 * mid] = cotan_low[:, mid:]

    @pl.when(jnp.logical_not(upper))
    def _():
        own_out[:, :mid] = normed_low[:, mid:]
        own_out[:, mid : 2 * mid] = cotan_low[:, mid:]
        far_out[:, :mid] = normed_low[:, :mid]
        far_out[:, mid : 2 * mid] = cotan_low[:, :mid]


def load_kernel(chunks, source, target, sems):
    step = source.shape[0] // chunks
    copies = [
        pltpu.make_async_copy(source.at[pl.ds(i * step, step)], target.at[pl.ds(i * step, step)], sems.at[i])
        for i in range(chunks)
    ]
    for copy in copies:
        copy.start()
    for copy in copies:
        copy.wait()


def loaded(weights, chunks):
    size = weights.size * weights.dtype.itemsize
    return pl.pallas_call(
        functools.partial(load_kernel, chunks),
        out_shape=jax.ShapeDtypeStruct(weights.shape, weights.dtype),
        in_specs=[pl.BlockSpec(memory_space=pl.ANY)],
        out_specs=VMEM,
        scratch_shapes=[pltpu.SemaphoreType.DMA((chunks,))],
        compiler_params=pltpu.CompilerParams(vmem_limit_bytes=max(4 << 20, 2 * size)),
        cost_estimate=pl.CostEstimate(flops=0, bytes_accessed=3 * size, transcendentals=0),
    )(weights)


def outer_kernel(chunks, own, far, first_out, second_out, pair, first, second, sems):
    rows, (mid, units) = own.shape[0], first.shape
    pair[:rows] = own[...]
    pair[rows:] = far[...]
    value = pair[:, 2 * mid : 2 * mid + units]
    d_hidden = pair[:, 2 * mid + units :]
    copies = []
    step = mid // chunks
    for i in range(chunks):
        part = slice(i * step, (i + 1) * step)
        first[part] = dot(pair[:, part], d_hidden, (0, 0)).astype(first.dtype)
        copies.append(pltpu.make_async_copy(first.at[part], first_out.at[part], sems.at[0, i]))
        copies[-1].start()
    for i in range(chunks):
        part = slice(i * step, (i + 1) * step)
        second[:, part] = dot(value, pair[:, mid + i * step : mid + (i + 1) * step], (0, 0)).astype(second.dtype)
        copies.append(pltpu.make_async_copy(second.at[:, part], second_out.at[:, part], sems.at[1, i]))
        copies[-1].start()
    for copy in copies:
        copy.wait()


def tail_kernel(rows, part, came, gain, tail, tail_rstd, fwd_out, bwd_out):
    f32 = jnp.float32
    branch = part[0, :rows] + came[:rows].astype(f32)
    fwd_out[...] = (tail[0] + branch).astype(fwd_out.dtype)
    scaled = (part[1, :rows] + came[rows:].astype(f32)) * gain[...]
    nhat = tail[2]
    d_input = tail_rstd[:, :1] * (
        scaled
        - jnp.mean(scaled, axis=-1, keepdims=True)
        - nhat * jnp.mean(scaled * nhat, axis=-1, keepdims=True)
    )
    bwd_out[...] = (tail[1] + d_input).astype(bwd_out.dtype)


def on_device(sent_fwd, sent_bwd, stash, gain, w_in, w_out):
    sections, mirrors = lax.axis_size("section"), lax.axis_size("mirror")
    count = lax.axis_size("dp")
    bits = count.bit_length() - 1
    masks = [(1 << bit) | 1 for bit in range(bits - 1, 0, -1)]
    rows, width = sent_fwd.shape[2], sent_fwd.shape[3]
    units = w_in.shape[2]
    fwd_in = lax.ppermute(sent_fwd[0, 0], AXES, relay_pairs(sections, mirrors, count, 1, 1))
    bwd_in = lax.ppermute(sent_bwd[0, 0], AXES, relay_pairs(sections, mirrors, count, 1, -1))
    w_first = loaded(w_in[0], 4)
    fwd_in, bwd_in, w_first = lax.optimization_barrier((fwd_in, bwd_in, w_first))
    w_second = loaded(w_out[0], 4)
    held = jnp.stack([fwd_in, bwd_in, stash[0, 0]])
    for mask in masks:
        flat = held.reshape(-1, width) if held.shape[1] == 1 else held
        other = lax.ppermute(flat, "dp", xor_pairs(count, mask)).reshape(held.shape)
        if mask == masks[0]:
            other, w_second = lax.optimization_barrier((other, w_second))
        held = jnp.concatenate([held, other], axis=1)
    other = lax.ppermute(held, "dp", xor_pairs(count, 1))
    half = held.shape[1]
    low = jax.ShapeDtypeStruct((2 * half, width + 2 * units), jnp.bfloat16)
    send, keep, own, away, tail, tail_rstd = pl.pallas_call(
        functools.partial(block_kernel, rows),
        out_shape=(
            jax.ShapeDtypeStruct((2, half, width), jnp.bfloat16),
            jax.ShapeDtypeStruct((2, half, width), jnp.float32),
            low,
            low,
            jax.ShapeDtypeStruct((3, rows, width), jnp.float32),
            jax.ShapeDtypeStruct((rows, 128), jnp.float32),
        ),
        in_specs=[VMEM] * 5,
        out_specs=[VMEM] * 6,
        compiler_params=pltpu.CompilerParams(vmem_limit_bytes=max(8 << 20, 40 * half * width * 4)),
    )(held, other, gain, w_first, w_second)
    part = None
    for mask in [1] + masks[::-1]:
        if part is not None:
            half = part.shape[1] // 2
            send, keep = part[:, half:].astype(jnp.bfloat16), part[:, :half]
        last = mask == (masks or [1])[0]
        came = lax.ppermute(send.reshape(-1, width) if last else send, "dp", xor_pairs(count, mask))
        if not last:
            part = keep + came.astype(jnp.float32)
            if mask == 1:
                part, away = lax.optimization_barrier((part, away))
    far = lax.ppermute(away, "mirror", xor_pairs(mirrors, 1))
    mid = width // 2
    grad_first, grad_second = pl.pallas_call(
        functools.partial(outer_kernel, 8),
        out_shape=(
            jax.ShapeDtypeStruct((mid, units), jnp.bfloat16),
            jax.ShapeDtypeStruct((units, mid), jnp.bfloat16),
        ),
        in_specs=[VMEM] * 2,
        out_specs=[pl.BlockSpec(memory_space=pl.ANY)] * 2,
        scratch_shapes=[
            pltpu.VMEM((2 * own.shape[0], own.shape[1]), jnp.bfloat16),
            pltpu.VMEM((mid, units), jnp.bfloat16),
            pltpu.VMEM((units, mid), jnp.bfloat16),
            pltpu.SemaphoreType.DMA((2, 8)),
        ],
        compiler_params=pltpu.CompilerParams(vmem_limit_bytes=max(6 << 20, 24 * own.size)),
        cost_estimate=pl.CostEstimate(flops=0, bytes_accessed=8 * mid * units, transcendentals=0),
    )(own, far)
    part, grad_first, grad_second = lax.optimization_barrier((part, grad_first, grad_second))
    fwd_out, bwd_out = pl.pallas_call(
        functools.partial(tail_kernel, rows),
        out_shape=(jax.ShapeDtypeStruct((rows, width), jnp.bfloat16),) * 2,
        in_specs=[VMEM] * 5,
        out_specs=[VMEM] * 2,
        compiler_params=pltpu.CompilerParams(vmem_limit_bytes=max(4 << 20, 40 * rows * width * 4)),
    )(part, came, gain, tail, tail_rstd)
    return (fwd_out[None, None], bwd_out[None, None], grad_first[None], grad_second[None])


def solution(mesh):
    in_specs = (
        P("section", "mirror", "dp", None),
        P("section", "mirror", "dp", None),
        P("section", "mirror", "dp", None),
        P("section", None),
        P("section", None, "dp"),
        P("section", "dp", None),
    )
    out_specs = (
        P("section", "mirror", "dp", None),
        P("section", "mirror", "dp", None),
        P("section", "mirror", "dp"),
        P("section", "dp", "mirror"),
    )
    return jax.shard_map(
        on_device, mesh=mesh, in_specs=in_specs, out_specs=out_specs, check_vma=False
    )
```

```python
import functools

import jax
import jax.numpy as jnp
from jax import lax
from jax.experimental import pallas as pl
from jax.experimental.pallas import tpu as pltpu
from jax.sharding import PartitionSpec as P

AXES = ("section", "mirror", "dp")
VMEM = pl.BlockSpec(memory_space=pltpu.VMEM)


def xor_pairs(count, mask):
    return [(source, source ^ mask) for source in range(count)]


def relay_pairs(sections, mirrors, count, mask, sign):
    pairs = []
    for section in range(sections):
        for mirror in range(mirrors):
            step = sign if mirror == 0 else -sign
            for dp in range(count):
                source = (section * mirrors + mirror) * count + dp
                target = ((section + step) % sections * mirrors + mirror) * count + (dp ^ mask)
                pairs.append((source, target))
    return sorted(pairs)


def norm_rows(x):
    centre = x - jnp.mean(x, axis=-1, keepdims=True)
    rstd = lax.rsqrt(jnp.mean(centre * centre, axis=-1, keepdims=True) + 1e-05)
    return (centre * rstd, rstd)


def gelu_pair(h):
    coeff = 0.7978845608028654
    inner = coeff * (h + 0.044715 * h * h * h)
    tanh_val = jnp.tanh(inner)
    value = 0.5 * h * (1.0 + tanh_val)
    slope = 0.5 * (1.0 + tanh_val) + 0.5 * h * (1.0 - tanh_val * tanh_val) * coeff * (
        1.0 + 3.0 * 0.044715 * h * h
    )
    return (value, slope)


def dot(left, right, contract):
    return lax.dot_general(left, right, ((contract[:1], contract[1:]), ((), ())), preferred_element_type=jnp.float32)


def block_kernel(rows, held, other, gain, wide, tall, send, keep, full, leaving):
    half, width = held.shape[1], held.shape[2]
    count, units = 2 * half, wide.shape[1] // 2
    f32, bf16 = jnp.float32, jnp.bfloat16

    def joined(first, second):
        return jnp.concatenate([first.astype(f32), second.astype(f32)], axis=0)

    cotan = joined(other[1], held[1]).astype(bf16)
    d_acted = dot(cotan, wide[:, :units], (1, 0))
    nhat_fwd, _ = norm_rows(joined(other[0], held[0]))
    nhat_bwd, _ = norm_rows(joined(held[2], other[2]))
    normed_bwd = nhat_bwd * gain[...]
    entering = jnp.concatenate([nhat_fwd * gain[...], normed_bwd], axis=0).astype(bf16)
    hidden = dot(entering, wide[:, units:], (1, 0))
    value, slope = gelu_pair(hidden)
    d_hidden = d_acted * slope[count:]
    leaving[...] = jnp.zeros_like(leaving)
    for slot in range(count // rows):
        source = slice(slot * rows, (slot + 1) * rows)
        leaving[2 * slot * rows : (2 * slot + 1) * rows, :units] = value[source]
        leaving[(2 * slot + 1) * rows : (2 * slot + 2) * rows, units:] = d_hidden[source]
    part = dot(leaving[...].astype(bf16), tall[...], (1, 0))
    send[...] = part[count:].astype(bf16)
    keep[...] = part[:count]
    full[:, :width] = normed_bwd.astype(bf16)
    full[:, width : 2 * width] = cotan
    full[:, 2 * width : 2 * width + units] = value[count:].astype(bf16)
    full[:, 2 * width + units :] = d_hidden.astype(bf16)


def side_kernel(rows, held, other, full, away, tail, tail_rstd):
    f32 = jnp.float32
    width = held.shape[2]
    mid = width // 2
    away[:, width:] = full[:, 2 * width :]
    upper = lax.axis_index("mirror") == 0

    @pl.when(upper)
    def _():
        away[:, :mid] = full[:, mid:width]
        away[:, mid:width] = full[:, width + mid : 2 * width]

    @pl.when(jnp.logical_not(upper))
    def _():
        away[:, :mid] = full[:, :mid]
        away[:, mid:width] = full[:, width : width + mid]

    nhat, rstd = norm_rows(held[2, :rows].astype(f32))
    tail[0] = other[0, :rows].astype(f32)
    tail[1] = other[1, :rows].astype(f32)
    tail[2] = nhat
    tail_rstd[...] = jnp.broadcast_to(rstd, tail_rstd.shape)


def load_kernel(chunks, source, target, sems):
    step = source.shape[0] // chunks
    copies = [
        pltpu.make_async_copy(source.at[pl.ds(i * step, step)], target.at[pl.ds(i * step, step)], sems.at[i])
        for i in range(chunks)
    ]
    for copy in copies:
        copy.start()
    for copy in copies:
        copy.wait()


def loaded(weights, chunks):
    size = weights.size * weights.dtype.itemsize
    return pl.pallas_call(
        functools.partial(load_kernel, chunks),
        out_shape=jax.ShapeDtypeStruct(weights.shape, weights.dtype),
        in_specs=[pl.BlockSpec(memory_space=pl.ANY)],
        out_specs=VMEM,
        scratch_shapes=[pltpu.SemaphoreType.DMA((chunks,))],
        compiler_params=pltpu.CompilerParams(vmem_limit_bytes=max(4 << 20, 2 * size)),
        cost_estimate=pl.CostEstimate(flops=0, bytes_accessed=3 * size, transcendentals=0),
    )(weights)


def prepare_kernel(w_in, w_out, wide, tall):
    units = w_in.shape[1]
    first, second = w_in[...], w_out[...]
    tall[:units] = second
    tall[units:] = first.T
    wide[:, :units] = second.T
    wide[:, units:] = first


def prepared(w_in, w_out):
    width, units = w_in.shape
    size = w_in.size * w_in.dtype.itemsize
    return pl.pallas_call(
        prepare_kernel,
        out_shape=(
            jax.ShapeDtypeStruct((width, 2 * units), w_in.dtype),
            jax.ShapeDtypeStruct((2 * units, width), w_in.dtype),
        ),
        in_specs=[VMEM] * 2,
        out_specs=[VMEM] * 2,
        compiler_params=pltpu.CompilerParams(vmem_limit_bytes=max(4 << 20, 10 * size)),
        cost_estimate=pl.CostEstimate(flops=0, bytes_accessed=4 * size, transcendentals=0),
    )(w_in, w_out)


def outer_kernel(chunks, full, far, first_out, second_out, pair, first, second, sems):
    rows, (mid, units) = far.shape[0], first.shape
    width = 2 * mid
    pair[rows:] = far[...]
    pair[:rows, width:] = full[:, 2 * width :]
    upper = lax.axis_index("mirror") == 0

    @pl.when(upper)
    def _():
        pair[:rows, :mid] = full[:, :mid]
        pair[:rows, mid:width] = full[:, width : width + mid]

    @pl.when(jnp.logical_not(upper))
    def _():
        pair[:rows, :mid] = full[:, mid:width]
        pair[:rows, mid:width] = full[:, width + mid : 2 * width]

    value = pair[:, 2 * mid : 2 * mid + units]
    d_hidden = pair[:, 2 * mid + units :]
    copies = []
    step = mid // chunks
    for i in range(chunks):
        part = slice(i * step, (i + 1) * step)
        first[part] = dot(pair[:, part], d_hidden, (0, 0)).astype(first.dtype)
        copies.append(pltpu.make_async_copy(first.at[part], first_out.at[part], sems.at[0, i]))
        copies[-1].start()
    for i in range(chunks):
        part = slice(i * step, (i + 1) * step)
        second[:, part] = dot(value, pair[:, mid + i * step : mid + (i + 1) * step], (0, 0)).astype(second.dtype)
        copies.append(pltpu.make_async_copy(second.at[:, part], second_out.at[:, part], sems.at[1, i]))
        copies[-1].start()
    for copy in copies:
        copy.wait()


def tail_kernel(rows, part, came, gain, tail, tail_rstd, fwd_out, bwd_out):
    f32 = jnp.float32
    branch = part[:rows] + came[:rows].astype(f32)
    fwd_out[...] = (tail[0] + branch).astype(fwd_out.dtype)
    scaled = (part[rows : 2 * rows] + came[rows:].astype(f32)) * gain[...]
    nhat = tail[2]
    d_input = tail_rstd[:, :1] * (
        scaled
        - jnp.mean(scaled, axis=-1, keepdims=True)
        - nhat * jnp.mean(scaled * nhat, axis=-1, keepdims=True)
    )
    bwd_out[...] = (tail[1] + d_input).astype(bwd_out.dtype)


def on_device(sent_fwd, sent_bwd, stash, gain, w_in, w_out):
    sections, mirrors = lax.axis_size("section"), lax.axis_size("mirror")
    count = lax.axis_size("dp")
    bits = count.bit_length() - 1
    masks = [(1 << bit) | 1 for bit in range(bits - 1, 0, -1)]
    rows, width = sent_fwd.shape[2], sent_fwd.shape[3]
    units = w_in.shape[2]
    fwd_in = lax.ppermute(sent_fwd[0, 0], AXES, relay_pairs(sections, mirrors, count, 1, 1))
    bwd_in = lax.ppermute(sent_bwd[0, 0], AXES, relay_pairs(sections, mirrors, count, 1, -1))
    w_first = loaded(w_in[0], 4)
    fwd_in, bwd_in, w_first = lax.optimization_barrier((fwd_in, bwd_in, w_first))
    w_second = loaded(w_out[0], 4)
    wide, tall = prepared(w_first, w_second)
    held = jnp.stack([fwd_in, bwd_in, stash[0, 0]])
    for mask in masks:
        flat = held.reshape(-1, width) if held.shape[1] == 1 else held
        other = lax.ppermute(flat, "dp", xor_pairs(count, mask)).reshape(held.shape)
        if mask == masks[0]:
            other, wide, tall = lax.optimization_barrier((other, wide, tall))
        held = jnp.concatenate([held, other], axis=1)
    other = lax.ppermute(held, "dp", xor_pairs(count, 1))
    half = held.shape[1]
    limit = pltpu.CompilerParams(vmem_limit_bytes=max(8 << 20, 40 * half * width * 4))
    send, keep, full = pl.pallas_call(
        functools.partial(block_kernel, rows),
        out_shape=(
            jax.ShapeDtypeStruct((2 * half, width), jnp.bfloat16),
            jax.ShapeDtypeStruct((2 * half, width), jnp.float32),
            jax.ShapeDtypeStruct((2 * half, 2 * width + 2 * units), jnp.bfloat16),
        ),
        in_specs=[VMEM] * 5,
        out_specs=[VMEM] * 3,
        scratch_shapes=[pltpu.VMEM((4 * half, 2 * units), jnp.float32)],
        compiler_params=limit,
    )(held, other, gain, wide, tall)
    away, tail, tail_rstd = pl.pallas_call(
        functools.partial(side_kernel, rows),
        out_shape=(
            jax.ShapeDtypeStruct((2 * half, width + 2 * units), jnp.bfloat16),
            jax.ShapeDtypeStruct((3, rows, width), jnp.float32),
            jax.ShapeDtypeStruct((rows, 128), jnp.float32),
        ),
        in_specs=[VMEM] * 3,
        out_specs=[VMEM] * 3,
        compiler_params=pltpu.CompilerParams(vmem_limit_bytes=max(4 << 20, 40 * rows * width * 4)),
    )(held, other, full)
    scatter = [1] + masks[::-1]
    for step, mask in enumerate(scatter):
        came = lax.ppermute(send, "dp", xor_pairs(count, mask))
        if step + 1 < len(scatter):
            part = keep + came.astype(jnp.float32)
            if step == 0:
                part, away, tail, tail_rstd = lax.optimization_barrier((part, away, tail, tail_rstd))
            half = part.shape[0] // 2
            send, keep = part[half:].astype(jnp.bfloat16), part[:half]
    far = lax.ppermute(away, "mirror", xor_pairs(mirrors, 1))
    mid = width // 2
    grad_first, grad_second = pl.pallas_call(
        functools.partial(outer_kernel, 8),
        out_shape=(
            jax.ShapeDtypeStruct((mid, units), jnp.bfloat16),
            jax.ShapeDtypeStruct((units, mid), jnp.bfloat16),
        ),
        in_specs=[VMEM] * 2,
        out_specs=[pl.BlockSpec(memory_space=pl.ANY)] * 2,
        scratch_shapes=[
            pltpu.VMEM((2 * far.shape[0], far.shape[1]), jnp.bfloat16),
            pltpu.VMEM((mid, units), jnp.bfloat16),
            pltpu.VMEM((units, mid), jnp.bfloat16),
            pltpu.SemaphoreType.DMA((2, 8)),
        ],
        compiler_params=pltpu.CompilerParams(vmem_limit_bytes=max(6 << 20, 24 * far.size)),
        cost_estimate=pl.CostEstimate(flops=0, bytes_accessed=8 * mid * units, transcendentals=0),
    )(full, far)
    part, grad_first, grad_second = lax.optimization_barrier((part, grad_first, grad_second))
    fwd_out, bwd_out = pl.pallas_call(
        functools.partial(tail_kernel, rows),
        out_shape=(jax.ShapeDtypeStruct((rows, width), jnp.bfloat16),) * 2,
        in_specs=[VMEM] * 5,
        out_specs=[VMEM] * 2,
        compiler_params=pltpu.CompilerParams(vmem_limit_bytes=max(4 << 20, 40 * rows * width * 4)),
    )(part, came, gain, tail, tail_rstd)
    return (fwd_out[None, None], bwd_out[None, None], grad_first[None], grad_second[None])


def solution(mesh):
    in_specs = (
        P("section", "mirror", "dp", None),
        P("section", "mirror", "dp", None),
        P("section", "mirror", "dp", None),
        P("section", None),
        P("section", None, "dp"),
        P("section", "dp", None),
    )
    out_specs = (
        P("section", "mirror", "dp", None),
        P("section", "mirror", "dp", None),
        P("section", "mirror", "dp"),
        P("section", "dp", "mirror"),
    )
    return jax.shard_map(
        on_device, mesh=mesh, in_specs=in_specs, out_specs=out_specs, check_vma=False
    )
```

```python
import functools

import jax
import jax.numpy as jnp
from jax import lax
from jax.experimental import pallas as pl
from jax.experimental.pallas import tpu as pltpu
from jax.sharding import PartitionSpec as P

AXES = ("section", "mirror", "dp")
VMEM = pl.BlockSpec(memory_space=pltpu.VMEM)


def xor_pairs(count, mask):
    return [(source, source ^ mask) for source in range(count)]


def relay_pairs(sections, mirrors, count, mask, sign):
    pairs = []
    for section in range(sections):
        for mirror in range(mirrors):
            step = sign if mirror == 0 else -sign
            for dp in range(count):
                source = (section * mirrors + mirror) * count + dp
                target = ((section + step) % sections * mirrors + mirror) * count + (dp ^ mask)
                pairs.append((source, target))
    return sorted(pairs)


def norm_rows(x):
    centre = x - jnp.mean(x, axis=-1, keepdims=True)
    rstd = lax.rsqrt(jnp.mean(centre * centre, axis=-1, keepdims=True) + 1e-05)
    return (centre * rstd, rstd)


def gelu_pair(h):
    coeff = 0.7978845608028654
    inner = coeff * (h + 0.044715 * h * h * h)
    tanh_val = jnp.tanh(inner)
    value = 0.5 * h * (1.0 + tanh_val)
    slope = 0.5 * (1.0 + tanh_val) + 0.5 * h * (1.0 - tanh_val * tanh_val) * coeff * (
        1.0 + 3.0 * 0.044715 * h * h
    )
    return (value, slope)


def dot(left, right, contract):
    return lax.dot_general(left, right, ((contract[:1], contract[1:]), ((), ())), preferred_element_type=jnp.float32)


def block_kernel(rows, held, gain, w_in, w_out_t, tall, send, keep, full, leaving):
    count, width = held.shape[1], held.shape[2]
    units = w_in.shape[1]
    f32, bf16 = jnp.float32, jnp.bfloat16
    cotan = held[1]
    d_acted = dot(cotan, w_out_t[...], (1, 0))
    nhat, _ = norm_rows(jnp.concatenate([held[0].astype(f32), held[2].astype(f32)], axis=0))
    normed = (nhat * gain[...]).astype(bf16)
    hidden = dot(normed, w_in[...], (1, 0))
    value, slope = gelu_pair(hidden)
    d_hidden = d_acted * slope[count:]
    leaving[...] = jnp.zeros_like(leaving)
    for slot in range(count // rows):
        source = slice(slot * rows, (slot + 1) * rows)
        leaving[2 * slot * rows : (2 * slot + 1) * rows, :units] = value[source]
        leaving[(2 * slot + 1) * rows : (2 * slot + 2) * rows, units:] = d_hidden[source]
    part = dot(leaving[...].astype(bf16), tall[...], (1, 0))
    send[...] = part[count:].astype(bf16)
    keep[...] = part[:count]
    full[:, :width] = (nhat[count:] * gain[...]).astype(bf16)
    full[:, width : 2 * width] = cotan
    low = units // 2
    value, d_hidden = value[count:].astype(bf16), d_hidden.astype(bf16)
    for side in range(2):
        start = 2 * width + 2 * side * low
        full[:, start : start + low] = value[:, side * low : (side + 1) * low]
        full[:, start + low : start + 2 * low] = d_hidden[:, side * low : (side + 1) * low]


def row_kernel(fwd_in, bwd_in, stash, tail, tail_rstd):
    nhat, rstd = norm_rows(stash[...].astype(jnp.float32))
    tail[0] = fwd_in[...].astype(jnp.float32)
    tail[1] = bwd_in[...].astype(jnp.float32)
    tail[2] = nhat
    tail_rstd[...] = jnp.broadcast_to(rstd, tail_rstd.shape)


def side_kernel(width, full, peer, own, away):
    count, low, mid = full.shape[0], own.shape[1] - width, width // 2
    upper = lax.axis_index("mirror") == 0
    for ref in (own, away):
        ref[:count, width:] = full[:, 2 * width : 2 * width + low]
        ref[count:, width:] = peer[:, 2 * width + low :]
    for source, target in ((full, slice(0, count)), (peer, slice(count, 2 * count))):

        @pl.when(upper)
        def _(source=source, target=target):
            own[target, :mid] = source[:, :mid]
            own[target, mid:width] = source[:, width : width + mid]
            away[target, :mid] = source[:, mid:width]
            away[target, mid:width] = source[:, width + mid : 2 * width]

        @pl.when(jnp.logical_not(upper))
        def _(source=source, target=target):
            own[target, :mid] = source[:, mid:width]
            own[target, mid:width] = source[:, width + mid : 2 * width]
            away[target, :mid] = source[:, :mid]
            away[target, mid:width] = source[:, width : width + mid]


def load_kernel(chunks, source, target, sems):
    step = source.shape[0] // chunks
    copies = [
        pltpu.make_async_copy(source.at[pl.ds(i * step, step)], target.at[pl.ds(i * step, step)], sems.at[i])
        for i in range(chunks)
    ]
    for copy in copies:
        copy.start()
    for copy in copies:
        copy.wait()


def loaded(weights, chunks):
    size = weights.size * weights.dtype.itemsize
    return pl.pallas_call(
        functools.partial(load_kernel, chunks),
        out_shape=jax.ShapeDtypeStruct(weights.shape, weights.dtype),
        in_specs=[pl.BlockSpec(memory_space=pl.ANY)],
        out_specs=VMEM,
        scratch_shapes=[pltpu.SemaphoreType.DMA((chunks,))],
        compiler_params=pltpu.CompilerParams(vmem_limit_bytes=max(4 << 20, 2 * size)),
        cost_estimate=pl.CostEstimate(flops=0, bytes_accessed=3 * size, transcendentals=0),
    )(weights)


def prepare_kernel(in_own, in_peer, out_own, out_peer, w_in, w_out_t, tall):
    low = in_own.shape[1]
    w_in[:, :low] = in_own[...]
    w_in[:, low:] = in_peer[...]
    w_out_t[:, :low] = out_own[...].T
    w_out_t[:, low:] = out_peer[...].T
    tall[:low] = out_own[...]
    tall[low : 2 * low] = out_peer[...]
    tall[2 * low : 3 * low] = in_own[...].T
    tall[3 * low :] = in_peer[...].T


def prepared(in_own, in_peer, out_own, out_peer):
    width, low = in_own.shape
    size = in_own.size * in_own.dtype.itemsize
    return pl.pallas_call(
        prepare_kernel,
        out_shape=(
            jax.ShapeDtypeStruct((width, 2 * low), in_own.dtype),
            jax.ShapeDtypeStruct((width, 2 * low), in_own.dtype),
            jax.ShapeDtypeStruct((4 * low, width), in_own.dtype),
        ),
        in_specs=[VMEM] * 4,
        out_specs=[VMEM] * 3,
        compiler_params=pltpu.CompilerParams(vmem_limit_bytes=max(4 << 20, 4 * size)),
        cost_estimate=pl.CostEstimate(flops=0, bytes_accessed=6 * size, transcendentals=0),
    )(in_own, in_peer, out_own, out_peer)


def outer_kernel(chunks, own, far, first_out, second_out, pair, first, second, sems):
    rows, (mid, units) = own.shape[0], first.shape
    pair[:rows] = own[...]
    pair[rows:] = far[...]
    value = pair[:, 2 * mid : 2 * mid + units]
    d_hidden = pair[:, 2 * mid + units :]
    copies = []
    step = mid // chunks
    for i in range(chunks):
        part = slice(i * step, (i + 1) * step)
        first[part] = dot(pair[:, part], d_hidden, (0, 0)).astype(first.dtype)
        copies.append(pltpu.make_async_copy(first.at[part], first_out.at[part], sems.at[0, i]))
        copies[-1].start()
    for i in range(chunks):
        part = slice(i * step, (i + 1) * step)
        second[:, part] = dot(value, pair[:, mid + i * step : mid + (i + 1) * step], (0, 0)).astype(second.dtype)
        copies.append(pltpu.make_async_copy(second.at[:, part], second_out.at[:, part], sems.at[1, i]))
        copies[-1].start()
    for copy in copies:
        copy.wait()


def tail_kernel(rows, part, came, gain, tail, tail_rstd, fwd_out, bwd_out):
    f32 = jnp.float32
    branch = part[:rows] + came[:rows].astype(f32)
    fwd_out[...] = (tail[0] + branch).astype(fwd_out.dtype)
    scaled = (part[rows : 2 * rows] + came[rows:].astype(f32)) * gain[...]
    nhat = tail[2]
    d_input = tail_rstd[:, :1] * (
        scaled
        - jnp.mean(scaled, axis=-1, keepdims=True)
        - nhat * jnp.mean(scaled * nhat, axis=-1, keepdims=True)
    )
    bwd_out[...] = (tail[1] + d_input).astype(bwd_out.dtype)


def on_device(sent_fwd, sent_bwd, stash, gain, w_in, w_out):
    sections, mirrors = lax.axis_size("section"), lax.axis_size("mirror")
    count = lax.axis_size("dp")
    bits = count.bit_length() - 1
    masks = [(1 << bit) | 1 for bit in range(bits - 1, 0, -1)]
    rows, width = sent_fwd.shape[2], sent_fwd.shape[3]
    units = w_in.shape[2]
    fwd_in = lax.ppermute(sent_fwd[0, 0], AXES, relay_pairs(sections, mirrors, count, 0, 1))
    bwd_in = lax.ppermute(sent_bwd[0, 0], AXES, relay_pairs(sections, mirrors, count, 0, -1))
    w_first = loaded(w_in[0], 4)
    fwd_in, bwd_in, w_first = lax.optimization_barrier((fwd_in, bwd_in, w_first))
    w_second = loaded(w_out[0], 4)
    peer_first = lax.ppermute(w_first, "dp", xor_pairs(count, 1))
    peer_second = lax.ppermute(w_second, "dp", xor_pairs(count, 1))
    tail, tail_rstd = pl.pallas_call(
        row_kernel,
        out_shape=(
            jax.ShapeDtypeStruct((3, rows, width), jnp.float32),
            jax.ShapeDtypeStruct((rows, 128), jnp.float32),
        ),
        in_specs=[VMEM] * 3,
        out_specs=[VMEM] * 2,
        compiler_params=pltpu.CompilerParams(vmem_limit_bytes=max(4 << 20, 40 * rows * width * 4)),
    )(fwd_in, bwd_in, stash[0, 0])
    held = jnp.stack([fwd_in, bwd_in, stash[0, 0]])
    for mask in masks:
        flat = held.reshape(-1, width) if held.shape[1] == 1 else held
        other = lax.ppermute(flat, "dp", xor_pairs(count, mask)).reshape(held.shape)
        if mask == masks[0]:
            other, w_second, tail, tail_rstd = lax.optimization_barrier((other, w_second, tail, tail_rstd))
            weights = prepared(w_first, peer_first, w_second, peer_second)
        if mask == masks[-1]:
            other, *weights = lax.optimization_barrier((other, *weights))
        held = jnp.concatenate([held, other], axis=1)
    half = held.shape[1]
    limit = pltpu.CompilerParams(vmem_limit_bytes=max(8 << 20, 40 * half * width * 4))
    send, keep, full = pl.pallas_call(
        functools.partial(block_kernel, rows),
        out_shape=(
            jax.ShapeDtypeStruct((half, width), jnp.bfloat16),
            jax.ShapeDtypeStruct((half, width), jnp.float32),
            jax.ShapeDtypeStruct((half, 2 * width + 4 * units), jnp.bfloat16),
        ),
        in_specs=[VMEM] * 5,
        out_specs=[VMEM] * 3,
        scratch_shapes=[pltpu.VMEM((2 * half, 4 * units), jnp.float32)],
        compiler_params=limit,
    )(held, gain, *weights)
    peer = lax.ppermute(full, "dp", xor_pairs(count, 1))
    low = jax.ShapeDtypeStruct((2 * half, width + 2 * units), jnp.bfloat16)
    own, away = pl.pallas_call(
        functools.partial(side_kernel, width),
        out_shape=(low, low),
        in_specs=[VMEM] * 2,
        out_specs=[VMEM] * 2,
        compiler_params=pltpu.CompilerParams(vmem_limit_bytes=4 << 20),
    )(full, peer)
    scatter = masks[::-1]
    for step, mask in enumerate(scatter):
        came = lax.ppermute(send, "dp", xor_pairs(count, mask))
        if step + 1 < len(scatter):
            part = keep + came.astype(jnp.float32)
            half = part.shape[0] // 2
            send, keep = part[half:].astype(jnp.bfloat16), part[:half]
    far = lax.ppermute(away, "mirror", xor_pairs(mirrors, 1))
    mid = width // 2
    grad_first, grad_second = pl.pallas_call(
        functools.partial(outer_kernel, 8),
        out_shape=(
            jax.ShapeDtypeStruct((mid, units), jnp.bfloat16),
            jax.ShapeDtypeStruct((units, mid), jnp.bfloat16),
        ),
        in_specs=[VMEM] * 2,
        out_specs=[pl.BlockSpec(memory_space=pl.ANY)] * 2,
        scratch_shapes=[
            pltpu.VMEM((2 * far.shape[0], far.shape[1]), jnp.bfloat16),
            pltpu.VMEM((mid, units), jnp.bfloat16),
            pltpu.VMEM((units, mid), jnp.bfloat16),
            pltpu.SemaphoreType.DMA((2, 8)),
        ],
        compiler_params=pltpu.CompilerParams(vmem_limit_bytes=max(6 << 20, 24 * far.size)),
        cost_estimate=pl.CostEstimate(flops=0, bytes_accessed=8 * mid * units, transcendentals=0),
    )(own, far)
    part, grad_first, grad_second = lax.optimization_barrier((part, grad_first, grad_second))
    fwd_out, bwd_out = pl.pallas_call(
        functools.partial(tail_kernel, rows),
        out_shape=(jax.ShapeDtypeStruct((rows, width), jnp.bfloat16),) * 2,
        in_specs=[VMEM] * 5,
        out_specs=[VMEM] * 2,
        compiler_params=pltpu.CompilerParams(vmem_limit_bytes=max(4 << 20, 40 * rows * width * 4)),
    )(part, came, gain, tail, tail_rstd)
    return (fwd_out[None, None], bwd_out[None, None], grad_first[None], grad_second[None])


def solution(mesh):
    in_specs = (
        P("section", "mirror", "dp", None),
        P("section", "mirror", "dp", None),
        P("section", "mirror", "dp", None),
        P("section", None),
        P("section", None, "dp"),
        P("section", "dp", None),
    )
    out_specs = (
        P("section", "mirror", "dp", None),
        P("section", "mirror", "dp", None),
        P("section", "mirror", "dp"),
        P("section", "dp", "mirror"),
    )
    return jax.shard_map(
        on_device, mesh=mesh, in_specs=in_specs, out_specs=out_specs, check_vma=False
    )
```

```python
import functools

import jax
import jax.numpy as jnp
from jax import lax
from jax.experimental import pallas as pl
from jax.experimental.pallas import tpu as pltpu
from jax.sharding import PartitionSpec as P

AXES = ("section", "mirror", "dp")
VMEM = pl.BlockSpec(memory_space=pltpu.VMEM)


def xor_pairs(count, mask):
    return [(source, source ^ mask) for source in range(count)]


def relay_pairs(sections, mirrors, count, mask, sign):
    pairs = []
    for section in range(sections):
        for mirror in range(mirrors):
            step = sign if mirror == 0 else -sign
            for dp in range(count):
                source = (section * mirrors + mirror) * count + dp
                target = ((section + step) % sections * mirrors + mirror) * count + (dp ^ mask)
                pairs.append((source, target))
    return sorted(pairs)


def norm_rows(x):
    centre = x - jnp.mean(x, axis=-1, keepdims=True)
    rstd = lax.rsqrt(jnp.mean(centre * centre, axis=-1, keepdims=True) + 1e-05)
    return (centre * rstd, rstd)


def gelu_pair(h):
    coeff = 0.7978845608028654
    inner = coeff * (h + 0.044715 * h * h * h)
    tanh_val = jnp.tanh(inner)
    value = 0.5 * h * (1.0 + tanh_val)
    slope = 0.5 * (1.0 + tanh_val) + 0.5 * h * (1.0 - tanh_val * tanh_val) * coeff * (
        1.0 + 3.0 * 0.044715 * h * h
    )
    return (value, slope)


def dot(left, right, contract):
    return lax.dot_general(left, right, ((contract[:1], contract[1:]), ((), ())), preferred_element_type=jnp.float32)


def block_kernel(rows, held, other, gain, w_in, w_out_t, tall, send, keep, full, leaving):
    count, width = 2 * held.shape[1], held.shape[2]
    units = w_in.shape[1]
    f32, bf16 = jnp.float32, jnp.bfloat16

    def joined(*arrays):
        return jnp.concatenate([piece[array].astype(f32) for array in arrays for piece in (held, other)], axis=0)

    cotan = joined(1).astype(bf16)
    d_acted = dot(cotan, w_out_t[...], (1, 0))
    nhat, _ = norm_rows(joined(0, 2))
    normed = (nhat * gain[...]).astype(bf16)
    hidden = dot(normed, w_in[...], (1, 0))
    value, slope = gelu_pair(hidden)
    d_hidden = d_acted * slope[count:]
    leaving[...] = jnp.zeros_like(leaving)
    for slot in range(count // rows):
        source = slice(slot * rows, (slot + 1) * rows)
        leaving[2 * slot * rows : (2 * slot + 1) * rows, :units] = value[source]
        leaving[(2 * slot + 1) * rows : (2 * slot + 2) * rows, units:] = d_hidden[source]
    part = dot(leaving[...].astype(bf16), tall[...], (1, 0))
    send[...] = part[count:].astype(bf16)
    keep[...] = part[:count]
    full[:, :width] = (nhat[count:] * gain[...]).astype(bf16)
    full[:, width : 2 * width] = cotan
    low = units // 2
    value, d_hidden = value[count:].astype(bf16), d_hidden.astype(bf16)
    for side in range(2):
        start = 2 * width + 2 * side * low
        full[:, start : start + low] = value[:, side * low : (side + 1) * low]
        full[:, start + low : start + 2 * low] = d_hidden[:, side * low : (side + 1) * low]


def row_kernel(stash, nhat_out, rstd_out):
    nhat, rstd = norm_rows(stash[...].astype(jnp.float32))
    nhat_out[...] = nhat
    rstd_out[...] = jnp.broadcast_to(rstd, rstd_out.shape)


def stack_kernel(rows, pair, stash, held):
    held[: 2 * rows] = pair[...]
    held[2 * rows :] = stash[...]


def merge_kernel(held, other, merged):
    count = merged.shape[1] // 2
    for array in range(3):
        pieces = [
            (ref[array] if len(ref.shape) == 3 else ref[array * count : (array + 1) * count]).astype(jnp.float32)
            for ref in (held, other)
        ]
        merged[array] = jnp.concatenate(pieces, axis=0).astype(merged.dtype)


def side_kernel(width, full, peer, own, away):
    count, low, mid = full.shape[0], own.shape[1] - width, width // 2
    upper = lax.axis_index("mirror") == 0
    for ref in (own, away):
        ref[:count, width:] = full[:, 2 * width : 2 * width + low]
        ref[count:, width:] = peer[:, 2 * width + low :]
    for source, target in ((full, slice(0, count)), (peer, slice(count, 2 * count))):

        @pl.when(upper)
        def _(source=source, target=target):
            own[target, :mid] = source[:, :mid]
            own[target, mid:width] = source[:, width : width + mid]
            away[target, :mid] = source[:, mid:width]
            away[target, mid:width] = source[:, width + mid : 2 * width]

        @pl.when(jnp.logical_not(upper))
        def _(source=source, target=target):
            own[target, :mid] = source[:, mid:width]
            own[target, mid:width] = source[:, width + mid : 2 * width]
            away[target, :mid] = source[:, :mid]
            away[target, mid:width] = source[:, width : width + mid]


def load_kernel(chunks, source, target, sems):
    step = source.shape[0] // chunks
    copies = [
        pltpu.make_async_copy(source.at[pl.ds(i * step, step)], target.at[pl.ds(i * step, step)], sems.at[i])
        for i in range(chunks)
    ]
    for copy in copies:
        copy.start()
    for copy in copies:
        copy.wait()


def loaded(weights, chunks):
    size = weights.size * weights.dtype.itemsize
    return pl.pallas_call(
        functools.partial(load_kernel, chunks),
        out_shape=jax.ShapeDtypeStruct(weights.shape, weights.dtype),
        in_specs=[pl.BlockSpec(memory_space=pl.ANY)],
        out_specs=VMEM,
        scratch_shapes=[pltpu.SemaphoreType.DMA((chunks,))],
        compiler_params=pltpu.CompilerParams(vmem_limit_bytes=max(4 << 20, 2 * size)),
        cost_estimate=pl.CostEstimate(flops=0, bytes_accessed=3 * size, transcendentals=0),
    )(weights)


def prepare_kernel(in_own, in_peer, out_own, out_peer, w_in, w_out_t, tall):
    low = in_own.shape[1]
    w_in[:, :low] = in_own[...]
    w_in[:, low:] = in_peer[...]
    w_out_t[:, :low] = out_own[...].T
    w_out_t[:, low:] = out_peer[...].T
    tall[:low] = out_own[...]
    tall[low : 2 * low] = out_peer[...]
    tall[2 * low : 3 * low] = in_own[...].T
    tall[3 * low :] = in_peer[...].T


def prepared(in_own, in_peer, out_own, out_peer):
    width, low = in_own.shape
    size = in_own.size * in_own.dtype.itemsize
    return pl.pallas_call(
        prepare_kernel,
        out_shape=(
            jax.ShapeDtypeStruct((width, 2 * low), in_own.dtype),
            jax.ShapeDtypeStruct((width, 2 * low), in_own.dtype),
            jax.ShapeDtypeStruct((4 * low, width), in_own.dtype),
        ),
        in_specs=[VMEM] * 4,
        out_specs=[VMEM] * 3,
        compiler_params=pltpu.CompilerParams(vmem_limit_bytes=max(4 << 20, 4 * size)),
        cost_estimate=pl.CostEstimate(flops=0, bytes_accessed=6 * size, transcendentals=0),
    )(in_own, in_peer, out_own, out_peer)


def outer_kernel(chunks, own, far, first_out, second_out, pair, first, second, sems):
    rows, (mid, units) = own.shape[0], first.shape
    pair[:rows] = own[...]
    pair[rows:] = far[...]
    value = pair[:, 2 * mid : 2 * mid + units]
    d_hidden = pair[:, 2 * mid + units :]
    copies = []
    step = mid // chunks
    for i in range(chunks):
        part = slice(i * step, (i + 1) * step)
        first[part] = dot(pair[:, part], d_hidden, (0, 0)).astype(first.dtype)
        copies.append(pltpu.make_async_copy(first.at[part], first_out.at[part], sems.at[0, i]))
        copies[-1].start()
    for i in range(chunks):
        part = slice(i * step, (i + 1) * step)
        second[:, part] = dot(value, pair[:, mid + i * step : mid + (i + 1) * step], (0, 0)).astype(second.dtype)
        copies.append(pltpu.make_async_copy(second.at[:, part], second_out.at[:, part], sems.at[1, i]))
        copies[-1].start()
    for copy in copies:
        copy.wait()


def tail_kernel(rows, part, came, gain, pair, nhat_in, rstd, fwd_out, bwd_out):
    f32 = jnp.float32
    branch = part[:rows] + came[:rows].astype(f32)
    fwd_out[...] = (pair[:rows].astype(f32) + branch).astype(fwd_out.dtype)
    scaled = (part[rows : 2 * rows] + came[rows:].astype(f32)) * gain[...]
    nhat = nhat_in[...]
    d_input = rstd[:, :1] * (
        scaled
        - jnp.mean(scaled, axis=-1, keepdims=True)
        - nhat * jnp.mean(scaled * nhat, axis=-1, keepdims=True)
    )
    bwd_out[...] = (pair[rows:].astype(f32) + d_input).astype(bwd_out.dtype)


def on_device(sent_fwd, sent_bwd, stash, gain, w_in, w_out):
    sections, mirrors = lax.axis_size("section"), lax.axis_size("mirror")
    count = lax.axis_size("dp")
    bits = count.bit_length() - 1
    masks = [(1 << bit) | 1 for bit in range(bits - 1, 0, -1)]
    rows, width = sent_fwd.shape[2], sent_fwd.shape[3]
    units = w_in.shape[2]
    onward, back = [relay_pairs(sections, mirrors, count, 0, sign) for sign in (1, -1)]
    if onward == back:
        pair = jnp.concatenate([sent_fwd[0, 0], sent_bwd[0, 0]], axis=0)
        pair = lax.ppermute(pair, AXES, onward)
    else:
        fwd_in = lax.ppermute(sent_fwd[0, 0], AXES, onward)
        bwd_in = lax.ppermute(sent_bwd[0, 0], AXES, back)
        pair = jnp.concatenate([fwd_in, bwd_in], axis=0)
    nhat, rstd = pl.pallas_call(
        row_kernel,
        out_shape=(
            jax.ShapeDtypeStruct((rows, width), jnp.float32),
            jax.ShapeDtypeStruct((rows, 128), jnp.float32),
        ),
        in_specs=[VMEM],
        out_specs=[VMEM] * 2,
        compiler_params=pltpu.CompilerParams(vmem_limit_bytes=max(4 << 20, 40 * rows * width * 4)),
    )(stash[0, 0])
    w_second = loaded(w_out[0], 4)
    peer_second = lax.ppermute(w_second, "dp", xor_pairs(count, 1))
    pair, w_second, source = lax.optimization_barrier((pair, w_second, w_in[0]))
    peer_first = lax.ppermute(source, "dp", xor_pairs(count, 1))
    w_first = loaded(w_in[0], 4)
    held = pl.pallas_call(
        functools.partial(stack_kernel, rows),
        out_shape=jax.ShapeDtypeStruct((3 * rows, width), jnp.bfloat16),
        in_specs=[VMEM] * 2,
        out_specs=VMEM,
        compiler_params=pltpu.CompilerParams(vmem_limit_bytes=max(4 << 20, 24 * rows * width)),
    )(pair, stash[0, 0])
    slots = rows
    for mask in masks:
        other = lax.ppermute(held, "dp", xor_pairs(count, mask))
        if mask == masks[0]:
            weights = prepared(w_first, peer_first, w_second, peer_second)
        if mask == masks[-1]:
            other, *weights = lax.optimization_barrier((other, *weights))
            break
        slots *= 2
        held = pl.pallas_call(
            merge_kernel,
            out_shape=jax.ShapeDtypeStruct((3, slots, width), jnp.bfloat16),
            in_specs=[VMEM] * 2,
            out_specs=VMEM,
            compiler_params=pltpu.CompilerParams(vmem_limit_bytes=max(4 << 20, 48 * slots * width)),
        )(held, other)
        if mask == masks[0]:
            held, w_first, nhat, rstd = lax.optimization_barrier((held, w_first, nhat, rstd))
    half = 2 * slots
    limit = pltpu.CompilerParams(vmem_limit_bytes=max(8 << 20, 40 * half * width * 4))
    send, keep, full = pl.pallas_call(
        functools.partial(block_kernel, rows),
        out_shape=(
            jax.ShapeDtypeStruct((half, width), jnp.bfloat16),
            jax.ShapeDtypeStruct((half, width), jnp.float32),
            jax.ShapeDtypeStruct((half, 2 * width + 4 * units), jnp.bfloat16),
        ),
        in_specs=[VMEM] * 6,
        out_specs=[VMEM] * 3,
        scratch_shapes=[pltpu.VMEM((2 * half, 4 * units), jnp.float32)],
        compiler_params=limit,
    )(held, other, gain, *weights)
    peer = lax.ppermute(full, "dp", xor_pairs(count, 1))
    low = jax.ShapeDtypeStruct((2 * half, width + 2 * units), jnp.bfloat16)
    own, away = pl.pallas_call(
        functools.partial(side_kernel, width),
        out_shape=(low, low),
        in_specs=[VMEM] * 2,
        out_specs=[VMEM] * 2,
        compiler_params=pltpu.CompilerParams(vmem_limit_bytes=4 << 20),
    )(full, peer)
    scatter = masks[::-1]
    for step, mask in enumerate(scatter):
        came = lax.ppermute(send, "dp", xor_pairs(count, mask))
        if step + 1 < len(scatter):
            part = keep + came.astype(jnp.float32)
            half = part.shape[0] // 2
            send, keep = part[half:].astype(jnp.bfloat16), part[:half]
    far = lax.ppermute(away, "mirror", xor_pairs(mirrors, 1))
    mid = width // 2
    grad_first, grad_second = pl.pallas_call(
        functools.partial(outer_kernel, 8),
        out_shape=(
            jax.ShapeDtypeStruct((mid, units), jnp.bfloat16),
            jax.ShapeDtypeStruct((units, mid), jnp.bfloat16),
        ),
        in_specs=[VMEM] * 2,
        out_specs=[pl.BlockSpec(memory_space=pl.ANY)] * 2,
        scratch_shapes=[
            pltpu.VMEM((2 * far.shape[0], far.shape[1]), jnp.bfloat16),
            pltpu.VMEM((mid, units), jnp.bfloat16),
            pltpu.VMEM((units, mid), jnp.bfloat16),
            pltpu.SemaphoreType.DMA((2, 8)),
        ],
        compiler_params=pltpu.CompilerParams(vmem_limit_bytes=max(6 << 20, 24 * far.size)),
        cost_estimate=pl.CostEstimate(flops=0, bytes_accessed=8 * mid * units, transcendentals=0),
    )(own, far)
    part, grad_first, grad_second = lax.optimization_barrier((part, grad_first, grad_second))
    fwd_out, bwd_out = pl.pallas_call(
        functools.partial(tail_kernel, rows),
        out_shape=(jax.ShapeDtypeStruct((rows, width), jnp.bfloat16),) * 2,
        in_specs=[VMEM] * 6,
        out_specs=[VMEM] * 2,
        compiler_params=pltpu.CompilerParams(vmem_limit_bytes=max(4 << 20, 40 * rows * width * 4)),
    )(part, came, gain, pair, nhat, rstd)
    return (fwd_out[None, None], bwd_out[None, None], grad_first[None], grad_second[None])


def solution(mesh):
    in_specs = (
        P("section", "mirror", "dp", None),
        P("section", "mirror", "dp", None),
        P("section", "mirror", "dp", None),
        P("section", None),
        P("section", None, "dp"),
        P("section", "dp", None),
    )
    out_specs = (
        P("section", "mirror", "dp", None),
        P("section", "mirror", "dp", None),
        P("section", "mirror", "dp"),
        P("section", "dp", "mirror"),
    )
    return jax.shard_map(
        on_device, mesh=mesh, in_specs=in_specs, out_specs=out_specs, check_vma=False
    )
```

```python
import functools

import jax
import jax.numpy as jnp
from jax import lax
from jax.experimental import pallas as pl
from jax.experimental.pallas import tpu as pltpu
from jax.sharding import PartitionSpec as P

AXES = ("section", "mirror", "dp")
VMEM = pl.BlockSpec(memory_space=pltpu.VMEM)


def xor_pairs(count, mask):
    return [(source, source ^ mask) for source in range(count)]


def relay_pairs(sections, mirrors, count, mask, sign):
    pairs = []
    for section in range(sections):
        for mirror in range(mirrors):
            step = sign if mirror == 0 else -sign
            for dp in range(count):
                source = (section * mirrors + mirror) * count + dp
                target = ((section + step) % sections * mirrors + mirror) * count + (dp ^ mask)
                pairs.append((source, target))
    return sorted(pairs)


def norm_rows(x):
    centre = x - jnp.mean(x, axis=-1, keepdims=True)
    rstd = lax.rsqrt(jnp.mean(centre * centre, axis=-1, keepdims=True) + 1e-05)
    return (centre * rstd, rstd)


def gelu_pair(h):
    coeff = 0.7978845608028654
    inner = coeff * (h + 0.044715 * h * h * h)
    tanh_val = jnp.tanh(inner)
    value = 0.5 * h * (1.0 + tanh_val)
    slope = 0.5 * (1.0 + tanh_val) + 0.5 * h * (1.0 - tanh_val * tanh_val) * coeff * (
        1.0 + 3.0 * 0.044715 * h * h
    )
    return (value, slope)


def dot(left, right, contract):
    return lax.dot_general(left, right, ((contract[:1], contract[1:]), ((), ())), preferred_element_type=jnp.float32)


def of_array(ref, array):
    if len(ref.shape) == 3:
        return ref[array].astype(jnp.float32)
    rows = ref.shape[0] // 3
    return ref[array * rows : (array + 1) * rows].astype(jnp.float32)


def block_kernel(rows, outer, second, fourth, gain, w_in, w_out_t, tall, send, keep, full, leaving):
    count, width = keep.shape
    units = w_in.shape[1]
    f32, bf16 = jnp.float32, jnp.bfloat16

    def joined(*arrays):
        pieces = []
        for array in arrays:
            both = of_array(outer, array)
            near = both.shape[0] // 2
            pieces += [both[:near], of_array(second, array), both[near:], of_array(fourth, array)]
        return jnp.concatenate(pieces, axis=0)

    cotan = joined(1).astype(bf16)
    d_acted = dot(cotan, w_out_t[...], (1, 0))
    nhat, _ = norm_rows(joined(0, 2))
    normed = (nhat * gain[...]).astype(bf16)
    hidden = dot(normed, w_in[...], (1, 0))
    value, slope = gelu_pair(hidden)
    d_hidden = d_acted * slope[count:]
    leaving[...] = jnp.zeros_like(leaving)
    for slot in range(count // rows):
        source = slice(slot * rows, (slot + 1) * rows)
        leaving[2 * slot * rows : (2 * slot + 1) * rows, :units] = value[source]
        leaving[(2 * slot + 1) * rows : (2 * slot + 2) * rows, units:] = d_hidden[source]
    part = dot(leaving[...].astype(bf16), tall[...], (1, 0))
    send[...] = part[count:].astype(bf16)
    keep[...] = part[:count]
    full[:, :width] = (nhat[count:] * gain[...]).astype(bf16)
    full[:, width : 2 * width] = cotan
    low = units // 2
    value, d_hidden = value[count:].astype(bf16), d_hidden.astype(bf16)
    for side in range(2):
        start = 2 * width + 2 * side * low
        full[:, start : start + low] = value[:, side * low : (side + 1) * low]
        full[:, start + low : start + 2 * low] = d_hidden[:, side * low : (side + 1) * low]


def row_kernel(stash, nhat_out, rstd_out):
    nhat, rstd = norm_rows(stash[...].astype(jnp.float32))
    nhat_out[...] = nhat
    rstd_out[...] = jnp.broadcast_to(rstd, rstd_out.shape)


def stack_kernel(rows, pair, stash, held):
    held[: 2 * rows] = pair[...]
    held[2 * rows :] = stash[...]


def merge_kernel(held, other, merged):
    for array in range(3):
        pieces = [of_array(ref, array) for ref in (held, other)]
        merged[array] = jnp.concatenate(pieces, axis=0).astype(merged.dtype)


def side_kernel(width, full, peer, own, away):
    count, low, mid = full.shape[0], own.shape[1] - width, width // 2
    upper = lax.axis_index("mirror") == 0
    for ref in (own, away):
        ref[:count, width:] = full[:, 2 * width : 2 * width + low]
        ref[count:, width:] = peer[:, 2 * width + low :]
    for source, target in ((full, slice(0, count)), (peer, slice(count, 2 * count))):

        @pl.when(upper)
        def _(source=source, target=target):
            own[target, :mid] = source[:, :mid]
            own[target, mid:width] = source[:, width : width + mid]
            away[target, :mid] = source[:, mid:width]
            away[target, mid:width] = source[:, width + mid : 2 * width]

        @pl.when(jnp.logical_not(upper))
        def _(source=source, target=target):
            own[target, :mid] = source[:, mid:width]
            own[target, mid:width] = source[:, width + mid : 2 * width]
            away[target, :mid] = source[:, :mid]
            away[target, mid:width] = source[:, width : width + mid]


def load_kernel(chunks, source, target, sems):
    step = source.shape[0] // chunks
    copies = [
        pltpu.make_async_copy(source.at[pl.ds(i * step, step)], target.at[pl.ds(i * step, step)], sems.at[i])
        for i in range(chunks)
    ]
    for copy in copies:
        copy.start()
    for copy in copies:
        copy.wait()


def loaded(weights, chunks):
    size = weights.size * weights.dtype.itemsize
    return pl.pallas_call(
        functools.partial(load_kernel, chunks),
        out_shape=jax.ShapeDtypeStruct(weights.shape, weights.dtype),
        in_specs=[pl.BlockSpec(memory_space=pl.ANY)],
        out_specs=VMEM,
        scratch_shapes=[pltpu.SemaphoreType.DMA((chunks,))],
        compiler_params=pltpu.CompilerParams(vmem_limit_bytes=max(4 << 20, 2 * size)),
        cost_estimate=pl.CostEstimate(flops=0, bytes_accessed=3 * size, transcendentals=0),
    )(weights)


def prepare_kernel(in_own, in_peer, out_own, out_peer, w_in, w_out_t, tall):
    low = in_own.shape[1]
    w_in[:, :low] = in_own[...]
    w_in[:, low:] = in_peer[...]
    w_out_t[:, :low] = out_own[...].T
    w_out_t[:, low:] = out_peer[...].T
    tall[:low] = out_own[...]
    tall[low : 2 * low] = out_peer[...]
    tall[2 * low : 3 * low] = in_own[...].T
    tall[3 * low :] = in_peer[...].T


def prepared(in_own, in_peer, out_own, out_peer):
    width, low = in_own.shape
    size = in_own.size * in_own.dtype.itemsize
    return pl.pallas_call(
        prepare_kernel,
        out_shape=(
            jax.ShapeDtypeStruct((width, 2 * low), in_own.dtype),
            jax.ShapeDtypeStruct((width, 2 * low), in_own.dtype),
            jax.ShapeDtypeStruct((4 * low, width), in_own.dtype),
        ),
        in_specs=[VMEM] * 4,
        out_specs=[VMEM] * 3,
        compiler_params=pltpu.CompilerParams(vmem_limit_bytes=max(4 << 20, 4 * size)),
        cost_estimate=pl.CostEstimate(flops=0, bytes_accessed=6 * size, transcendentals=0),
    )(in_own, in_peer, out_own, out_peer)


def outer_kernel(chunks, own, far, first_out, second_out, pair, first, second, sems):
    rows, (mid, units) = own.shape[0], first.shape
    pair[:rows] = own[...]
    pair[rows:] = far[...]
    value = pair[:, 2 * mid : 2 * mid + units]
    d_hidden = pair[:, 2 * mid + units :]
    copies = []
    step = mid // chunks
    for i in range(chunks):
        part = slice(i * step, (i + 1) * step)
        first[part] = dot(pair[:, part], d_hidden, (0, 0)).astype(first.dtype)
        copies.append(pltpu.make_async_copy(first.at[part], first_out.at[part], sems.at[0, i]))
        copies[-1].start()
    for i in range(chunks):
        part = slice(i * step, (i + 1) * step)
        second[:, part] = dot(value, pair[:, mid + i * step : mid + (i + 1) * step], (0, 0)).astype(second.dtype)
        copies.append(pltpu.make_async_copy(second.at[:, part], second_out.at[:, part], sems.at[1, i]))
        copies[-1].start()
    for copy in copies:
        copy.wait()


def tail_kernel(rows, part, came, gain, pair, nhat_in, rstd, fwd_out, bwd_out):
    f32 = jnp.float32
    branch = part[:rows] + came[:rows].astype(f32)
    fwd_out[...] = (pair[:rows].astype(f32) + branch).astype(fwd_out.dtype)
    scaled = (part[rows : 2 * rows] + came[rows:].astype(f32)) * gain[...]
    nhat = nhat_in[...]
    d_input = rstd[:, :1] * (
        scaled
        - jnp.mean(scaled, axis=-1, keepdims=True)
        - nhat * jnp.mean(scaled * nhat, axis=-1, keepdims=True)
    )
    bwd_out[...] = (pair[rows:].astype(f32) + d_input).astype(bwd_out.dtype)


def on_device(sent_fwd, sent_bwd, stash, gain, w_in, w_out):
    sections, mirrors = lax.axis_size("section"), lax.axis_size("mirror")
    count = lax.axis_size("dp")
    bits = count.bit_length() - 1
    masks = [(1 << bit) | 1 for bit in range(bits - 1, 0, -1)]
    rows, width = sent_fwd.shape[2], sent_fwd.shape[3]
    units = w_in.shape[2]
    onward, back = [relay_pairs(sections, mirrors, count, 0, sign) for sign in (1, -1)]
    if onward == back:
        pair = jnp.concatenate([sent_fwd[0, 0], sent_bwd[0, 0]], axis=0)
        pair = lax.ppermute(pair, AXES, onward)
    else:
        fwd_in = lax.ppermute(sent_fwd[0, 0], AXES, onward)
        bwd_in = lax.ppermute(sent_bwd[0, 0], AXES, back)
        pair = jnp.concatenate([fwd_in, bwd_in], axis=0)
    nhat, rstd = pl.pallas_call(
        row_kernel,
        out_shape=(
            jax.ShapeDtypeStruct((rows, width), jnp.float32),
            jax.ShapeDtypeStruct((rows, 128), jnp.float32),
        ),
        in_specs=[VMEM],
        out_specs=[VMEM] * 2,
        compiler_params=pltpu.CompilerParams(vmem_limit_bytes=max(4 << 20, 40 * rows * width * 4)),
    )(stash[0, 0])
    peer_first, peer_second = [lax.ppermute(source, "dp", xor_pairs(count, 1)) for source in (w_in[0], w_out[0])]
    w_first = loaded(w_in[0], 4)
    pair, w_first = lax.optimization_barrier((pair, w_first))
    w_second = loaded(w_out[0], 4)
    held = pl.pallas_call(
        functools.partial(stack_kernel, rows),
        out_shape=jax.ShapeDtypeStruct((3 * rows, width), jnp.bfloat16),
        in_specs=[VMEM] * 2,
        out_specs=VMEM,
        compiler_params=pltpu.CompilerParams(vmem_limit_bytes=max(4 << 20, 24 * rows * width)),
        cost_estimate=pl.CostEstimate(flops=20 * 10**9, bytes_accessed=10**5, transcendentals=0),
    )(pair, stash[0, 0])
    slots = rows

    def from_peer(value, mask):
        return lax.ppermute(value, "dp", xor_pairs(count, mask))

    for mask in masks[:-2]:
        other = from_peer(held, mask)
        slots *= 2
        held = pl.pallas_call(
            merge_kernel,
            out_shape=jax.ShapeDtypeStruct((3, slots, width), jnp.bfloat16),
            in_specs=[VMEM] * 2,
            out_specs=VMEM,
            compiler_params=pltpu.CompilerParams(vmem_limit_bytes=max(4 << 20, 48 * slots * width)),
        )(held, other)
    second = from_peer(held, masks[-2])
    third = from_peer(held, masks[-1])
    second, w_second, nhat, rstd = lax.optimization_barrier((second, w_second, nhat, rstd))
    fourth = from_peer(second, masks[-1])
    weights = prepared(w_first, peer_first, w_second, peer_second)
    fourth, *weights = lax.optimization_barrier((fourth, *weights))
    slots *= 2
    outer = pl.pallas_call(
        merge_kernel,
        out_shape=jax.ShapeDtypeStruct((3, slots, width), jnp.bfloat16),
        in_specs=[VMEM] * 2,
        out_specs=VMEM,
        compiler_params=pltpu.CompilerParams(vmem_limit_bytes=max(4 << 20, 48 * slots * width)),
        cost_estimate=pl.CostEstimate(flops=10 * 10**9, bytes_accessed=10**5, transcendentals=0),
    )(held, third)
    half = 2 * slots
    limit = pltpu.CompilerParams(vmem_limit_bytes=max(8 << 20, 40 * half * width * 4))
    send, keep, full = pl.pallas_call(
        functools.partial(block_kernel, rows),
        out_shape=(
            jax.ShapeDtypeStruct((half, width), jnp.bfloat16),
            jax.ShapeDtypeStruct((half, width), jnp.float32),
            jax.ShapeDtypeStruct((half, 2 * width + 4 * units), jnp.bfloat16),
        ),
        in_specs=[VMEM] * 7,
        out_specs=[VMEM] * 3,
        scratch_shapes=[pltpu.VMEM((2 * half, 4 * units), jnp.float32)],
        compiler_params=limit,
    )(outer, second, fourth, gain, *weights)
    peer = lax.ppermute(full, "dp", xor_pairs(count, 1))
    low = jax.ShapeDtypeStruct((2 * half, width + 2 * units), jnp.bfloat16)
    own, away = pl.pallas_call(
        functools.partial(side_kernel, width),
        out_shape=(low, low),
        in_specs=[VMEM] * 2,
        out_specs=[VMEM] * 2,
        compiler_params=pltpu.CompilerParams(vmem_limit_bytes=4 << 20),
    )(full, peer)
    scatter = masks[::-1]
    for step, mask in enumerate(scatter):
        came = lax.ppermute(send, "dp", xor_pairs(count, mask))
        if step + 1 < len(scatter):
            part = keep + came.astype(jnp.float32)
            half = part.shape[0] // 2
            send, keep = part[half:].astype(jnp.bfloat16), part[:half]
    far = lax.ppermute(away, "mirror", xor_pairs(mirrors, 1))
    mid = width // 2
    grad_first, grad_second = pl.pallas_call(
        functools.partial(outer_kernel, 8),
        out_shape=(
            jax.ShapeDtypeStruct((mid, units), jnp.bfloat16),
            jax.ShapeDtypeStruct((units, mid), jnp.bfloat16),
        ),
        in_specs=[VMEM] * 2,
        out_specs=[pl.BlockSpec(memory_space=pl.ANY)] * 2,
        scratch_shapes=[
            pltpu.VMEM((2 * far.shape[0], far.shape[1]), jnp.bfloat16),
            pltpu.VMEM((mid, units), jnp.bfloat16),
            pltpu.VMEM((units, mid), jnp.bfloat16),
            pltpu.SemaphoreType.DMA((2, 8)),
        ],
        compiler_params=pltpu.CompilerParams(vmem_limit_bytes=max(6 << 20, 24 * far.size)),
        cost_estimate=pl.CostEstimate(flops=0, bytes_accessed=8 * mid * units, transcendentals=0),
    )(own, far)
    part, grad_first, grad_second = lax.optimization_barrier((part, grad_first, grad_second))
    fwd_out, bwd_out = pl.pallas_call(
        functools.partial(tail_kernel, rows),
        out_shape=(jax.ShapeDtypeStruct((rows, width), jnp.bfloat16),) * 2,
        in_specs=[VMEM] * 6,
        out_specs=[VMEM] * 2,
        compiler_params=pltpu.CompilerParams(vmem_limit_bytes=max(4 << 20, 40 * rows * width * 4)),
    )(part, came, gain, pair, nhat, rstd)
    return (fwd_out[None, None], bwd_out[None, None], grad_first[None], grad_second[None])


def solution(mesh):
    in_specs = (
        P("section", "mirror", "dp", None),
        P("section", "mirror", "dp", None),
        P("section", "mirror", "dp", None),
        P("section", None),
        P("section", None, "dp"),
        P("section", "dp", None),
    )
    out_specs = (
        P("section", "mirror", "dp", None),
        P("section", "mirror", "dp", None),
        P("section", "mirror", "dp"),
        P("section", "dp", "mirror"),
    )
    return jax.shard_map(
        on_device, mesh=mesh, in_specs=in_specs, out_specs=out_specs, check_vma=False
    )
```

```python
import functools

import jax
import jax.numpy as jnp
from jax import lax
from jax.experimental import pallas as pl
from jax.experimental.pallas import tpu as pltpu
from jax.sharding import PartitionSpec as P

AXES = ("section", "mirror", "dp")
VMEM = pl.BlockSpec(memory_space=pltpu.VMEM)


def xor_pairs(count, mask):
    return [(source, source ^ mask) for source in range(count)]


def relay_pairs(sections, mirrors, count, mask, sign):
    pairs = []
    for section in range(sections):
        for mirror in range(mirrors):
            step = sign if mirror == 0 else -sign
            for dp in range(count):
                source = (section * mirrors + mirror) * count + dp
                target = ((section + step) % sections * mirrors + mirror) * count + (dp ^ mask)
                pairs.append((source, target))
    return sorted(pairs)


def norm_rows(x):
    centre = x - jnp.mean(x, axis=-1, keepdims=True)
    rstd = lax.rsqrt(jnp.mean(centre * centre, axis=-1, keepdims=True) + 1e-05)
    return (centre * rstd, rstd)


def gelu_pair(h):
    coeff = 0.7978845608028654
    inner = coeff * (h + 0.044715 * h * h * h)
    tanh_val = jnp.tanh(inner)
    value = 0.5 * h * (1.0 + tanh_val)
    slope = 0.5 * (1.0 + tanh_val) + 0.5 * h * (1.0 - tanh_val * tanh_val) * coeff * (
        1.0 + 3.0 * 0.044715 * h * h
    )
    return (value, slope)


def dot(left, right, contract):
    return lax.dot_general(left, right, ((contract[:1], contract[1:]), ((), ())), preferred_element_type=jnp.float32)


def spread(ref, scratch, count):
    scratch[...] = ref[...].astype(jnp.float32)
    many = ref.shape[0] // count
    return jnp.concatenate([scratch[pl.ds(k, count, stride=many), :] for k in range(many)], axis=1)


def of_array(ref, array):
    if len(ref.shape) == 3:
        return ref[array].astype(jnp.float32)
    rows = ref.shape[0] // 3
    return ref[array * rows : (array + 1) * rows].astype(jnp.float32)


def block_kernel(rows, outer, fourth, gain, w_in, w_out_t, tall, send, keep, full, leaving, *scratch):
    count, width = keep.shape
    units = w_in.shape[1]
    f32, bf16 = jnp.float32, jnp.bfloat16

    last = spread(fourth, scratch[0], 3 * rows) if scratch else fourth

    def joined(*arrays):
        return jnp.concatenate([of_array(piece, array) for array in arrays for piece in (outer, last)], axis=0)

    cotan = joined(1).astype(bf16)
    d_acted = dot(cotan, w_out_t[...], (1, 0))
    nhat, _ = norm_rows(joined(0, 2))
    normed = (nhat * gain[...]).astype(bf16)
    hidden = dot(normed, w_in[...], (1, 0))
    value, slope = gelu_pair(hidden)
    d_hidden = d_acted * slope[count:]
    leaving[...] = jnp.zeros_like(leaving)
    for slot in range(count // rows):
        source = slice(slot * rows, (slot + 1) * rows)
        leaving[2 * slot * rows : (2 * slot + 1) * rows, :units] = value[source]
        leaving[(2 * slot + 1) * rows : (2 * slot + 2) * rows, units:] = d_hidden[source]
    part = dot(leaving[...].astype(bf16), tall[...], (1, 0))
    send[...] = part[count:].astype(bf16)
    keep[...] = part[:count]
    full[:, :width] = (nhat[count:] * gain[...]).astype(bf16)
    full[:, width : 2 * width] = cotan
    low = units // 2
    value, d_hidden = value[count:].astype(bf16), d_hidden.astype(bf16)
    for side in range(2):
        start = 2 * width + 2 * side * low
        full[:, start : start + low] = value[:, side * low : (side + 1) * low]
        full[:, start + low : start + 2 * low] = d_hidden[:, side * low : (side + 1) * low]


def row_kernel(stash, nhat_out, rstd_out):
    nhat, rstd = norm_rows(stash[...].astype(jnp.float32))
    nhat_out[...] = nhat
    rstd_out[...] = jnp.broadcast_to(rstd, rstd_out.shape)


def stack_kernel(rows, pair, stash, held, *scratch):
    if not scratch:
        held[: 2 * rows] = pair[...]
        held[2 * rows :] = stash[...]
        return
    step, many = held.shape[1], pair.shape[1] // held.shape[1]
    values = jnp.concatenate([pair[...].astype(jnp.float32), stash[...].astype(jnp.float32)], axis=0)
    for row in range(3 * rows):
        for k in range(many):
            scratch[0][many * row + k : many * row + k + 1] = values[row : row + 1, k * step : (k + 1) * step]
    held[...] = scratch[0][...].astype(held.dtype)


def merge_kernel(held, other, merged):
    for array in range(3):
        pieces = [of_array(ref, array) for ref in (held, other)]
        merged[array] = jnp.concatenate(pieces, axis=0).astype(merged.dtype)


def three_kernel(rows, held, second, third, merged, *scratch):
    refs = held, second, third
    if scratch:
        refs = [spread(ref, scratch[0].at[i], 3 * rows) for i, ref in enumerate(refs)]
    for array in range(3):
        pieces = [of_array(ref, array) for ref in refs]
        merged[array] = jnp.concatenate(pieces, axis=0).astype(merged.dtype)


def side_kernel(width, full, peer, own, away):
    count, low, mid = full.shape[0], own.shape[1] - width, width // 2
    upper = lax.axis_index("mirror") == 0
    for ref in (own, away):
        ref[:count, width:] = full[:, 2 * width : 2 * width + low]
        ref[count:, width:] = peer[:, 2 * width + low :]
    for source, target in ((full, slice(0, count)), (peer, slice(count, 2 * count))):

        @pl.when(upper)
        def _(source=source, target=target):
            own[target, :mid] = source[:, :mid]
            own[target, mid:width] = source[:, width : width + mid]
            away[target, :mid] = source[:, mid:width]
            away[target, mid:width] = source[:, width + mid : 2 * width]

        @pl.when(jnp.logical_not(upper))
        def _(source=source, target=target):
            own[target, :mid] = source[:, mid:width]
            own[target, mid:width] = source[:, width + mid : 2 * width]
            away[target, :mid] = source[:, :mid]
            away[target, mid:width] = source[:, width : width + mid]


def load_kernel(chunks, source, target, sems):
    step = source.shape[0] // chunks
    copies = [
        pltpu.make_async_copy(source.at[pl.ds(i * step, step)], target.at[pl.ds(i * step, step)], sems.at[i])
        for i in range(chunks)
    ]
    for copy in copies:
        copy.start()
    for copy in copies:
        copy.wait()


def loaded(weights, chunks):
    size = weights.size * weights.dtype.itemsize
    return pl.pallas_call(
        functools.partial(load_kernel, chunks),
        out_shape=jax.ShapeDtypeStruct(weights.shape, weights.dtype),
        in_specs=[pl.BlockSpec(memory_space=pl.ANY)],
        out_specs=VMEM,
        scratch_shapes=[pltpu.SemaphoreType.DMA((chunks,))],
        compiler_params=pltpu.CompilerParams(vmem_limit_bytes=max(4 << 20, 2 * size)),
        cost_estimate=pl.CostEstimate(flops=0, bytes_accessed=3 * size, transcendentals=0),
    )(weights)


def prepare_kernel(in_own, in_peer, out_own, out_peer, w_in, w_out_t, tall):
    low = in_own.shape[1]
    w_in[:, :low] = in_own[...]
    w_in[:, low:] = in_peer[...]
    w_out_t[:, :low] = out_own[...].T
    w_out_t[:, low:] = out_peer[...].T
    tall[:low] = out_own[...]
    tall[low : 2 * low] = out_peer[...]
    tall[2 * low : 3 * low] = in_own[...].T
    tall[3 * low :] = in_peer[...].T


def prepared(in_own, in_peer, out_own, out_peer):
    width, low = in_own.shape
    size = in_own.size * in_own.dtype.itemsize
    return pl.pallas_call(
        prepare_kernel,
        out_shape=(
            jax.ShapeDtypeStruct((width, 2 * low), in_own.dtype),
            jax.ShapeDtypeStruct((width, 2 * low), in_own.dtype),
            jax.ShapeDtypeStruct((4 * low, width), in_own.dtype),
        ),
        in_specs=[VMEM] * 4,
        out_specs=[VMEM] * 3,
        compiler_params=pltpu.CompilerParams(vmem_limit_bytes=max(4 << 20, 4 * size)),
        cost_estimate=pl.CostEstimate(flops=0, bytes_accessed=6 * size, transcendentals=0),
    )(in_own, in_peer, out_own, out_peer)


def outer_kernel(chunks, own, far, first_out, second_out, pair, first, second, sems):
    rows, (mid, units) = own.shape[0], first.shape
    pair[:rows] = own[...]
    pair[rows:] = far[...]
    value = pair[:, 2 * mid : 2 * mid + units]
    d_hidden = pair[:, 2 * mid + units :]
    copies = []
    step = mid // chunks
    for i in range(chunks):
        part = slice(i * step, (i + 1) * step)
        first[part] = dot(pair[:, part], d_hidden, (0, 0)).astype(first.dtype)
        copies.append(pltpu.make_async_copy(first.at[part], first_out.at[part], sems.at[0, i]))
        copies[-1].start()
    for i in range(chunks):
        part = slice(i * step, (i + 1) * step)
        second[:, part] = dot(value, pair[:, mid + i * step : mid + (i + 1) * step], (0, 0)).astype(second.dtype)
        copies.append(pltpu.make_async_copy(second.at[:, part], second_out.at[:, part], sems.at[1, i]))
        copies[-1].start()
    for copy in copies:
        copy.wait()


def tail_kernel(rows, part, came, gain, pair, nhat_in, rstd, fwd_out, bwd_out):
    f32 = jnp.float32
    branch = part[:rows] + came[:rows].astype(f32)
    fwd_out[...] = (pair[:rows].astype(f32) + branch).astype(fwd_out.dtype)
    scaled = (part[rows : 2 * rows] + came[rows:].astype(f32)) * gain[...]
    nhat = nhat_in[...]
    d_input = rstd[:, :1] * (
        scaled
        - jnp.mean(scaled, axis=-1, keepdims=True)
        - nhat * jnp.mean(scaled * nhat, axis=-1, keepdims=True)
    )
    bwd_out[...] = (pair[rows:].astype(f32) + d_input).astype(bwd_out.dtype)


def on_device(sent_fwd, sent_bwd, stash, gain, w_in, w_out):
    sections, mirrors = lax.axis_size("section"), lax.axis_size("mirror")
    count = lax.axis_size("dp")
    bits = count.bit_length() - 1
    masks = [(1 << bit) | 1 for bit in range(bits - 1, 0, -1)]
    rows, width = sent_fwd.shape[2], sent_fwd.shape[3]
    units = w_in.shape[2]
    onward, back = [relay_pairs(sections, mirrors, count, 0, sign) for sign in (1, -1)]
    if onward == back:
        pair = jnp.concatenate([sent_fwd[0, 0], sent_bwd[0, 0]], axis=0)
        pair = lax.ppermute(pair, AXES, onward)
    else:
        fwd_in = lax.ppermute(sent_fwd[0, 0], AXES, onward)
        bwd_in = lax.ppermute(sent_bwd[0, 0], AXES, back)
        pair = jnp.concatenate([fwd_in, bwd_in], axis=0)
    nhat, rstd = pl.pallas_call(
        row_kernel,
        out_shape=(
            jax.ShapeDtypeStruct((rows, width), jnp.float32),
            jax.ShapeDtypeStruct((rows, 128), jnp.float32),
        ),
        in_specs=[VMEM],
        out_specs=[VMEM] * 2,
        compiler_params=pltpu.CompilerParams(vmem_limit_bytes=max(4 << 20, 40 * rows * width * 4)),
    )(stash[0, 0])
    peer_first, peer_second = [lax.ppermute(source, "dp", xor_pairs(count, 1)) for source in (w_in[0], w_out[0])]
    w_first = loaded(w_in[0], 4)
    pair, w_first = lax.optimization_barrier((pair, w_first))
    w_second = loaded(w_out[0], 4)
    packed = len(masks) == 2 and width % 1024 == 0
    flat = (3 * rows * (width // 128), 128) if packed else (3 * rows, width)
    pieces = [pltpu.VMEM(flat, jnp.float32)] if packed else []
    held = pl.pallas_call(
        functools.partial(stack_kernel, rows),
        out_shape=jax.ShapeDtypeStruct(flat, jnp.bfloat16),
        in_specs=[VMEM] * 2,
        out_specs=VMEM,
        scratch_shapes=pieces,
        compiler_params=pltpu.CompilerParams(vmem_limit_bytes=max(4 << 20, 64 * rows * width)),
        cost_estimate=pl.CostEstimate(flops=20 * 10**9, bytes_accessed=10**5, transcendentals=0),
    )(pair, stash[0, 0])
    slots = rows

    def from_peer(value, mask):
        return lax.ppermute(value, "dp", xor_pairs(count, mask))

    for mask in masks[:-2]:
        other = from_peer(held, mask)
        slots *= 2
        held = pl.pallas_call(
            merge_kernel,
            out_shape=jax.ShapeDtypeStruct((3, slots, width), jnp.bfloat16),
            in_specs=[VMEM] * 2,
            out_specs=VMEM,
            compiler_params=pltpu.CompilerParams(vmem_limit_bytes=max(4 << 20, 48 * slots * width)),
        )(held, other)
    second = from_peer(held, masks[-2])
    third = from_peer(held, masks[-1])
    second, w_second, nhat, rstd = lax.optimization_barrier((second, w_second, nhat, rstd))
    fourth = from_peer(second, masks[-1])
    weights = prepared(w_first, peer_first, w_second, peer_second)
    fourth, *weights = lax.optimization_barrier((fourth, *weights))
    slots *= 2
    outer = pl.pallas_call(
        functools.partial(three_kernel, rows),
        out_shape=jax.ShapeDtypeStruct((3, slots // 2 * 3, width), jnp.bfloat16),
        in_specs=[VMEM] * 3,
        out_specs=VMEM,
        scratch_shapes=[pltpu.VMEM((3,) + flat, jnp.float32)] if packed else [],
        compiler_params=pltpu.CompilerParams(vmem_limit_bytes=max(4 << 20, 128 * slots * width)),
        cost_estimate=pl.CostEstimate(flops=10 * 10**9, bytes_accessed=10**5, transcendentals=0),
    )(held, second, third)
    half = 2 * slots
    limit = pltpu.CompilerParams(vmem_limit_bytes=max(8 << 20, 40 * half * width * 4))
    send, keep, full = pl.pallas_call(
        functools.partial(block_kernel, rows),
        out_shape=(
            jax.ShapeDtypeStruct((half, width), jnp.bfloat16),
            jax.ShapeDtypeStruct((half, width), jnp.float32),
            jax.ShapeDtypeStruct((half, 2 * width + 4 * units), jnp.bfloat16),
        ),
        in_specs=[VMEM] * 6,
        out_specs=[VMEM] * 3,
        scratch_shapes=[pltpu.VMEM((2 * half, 4 * units), jnp.float32)] + pieces,
        compiler_params=limit,
    )(outer, fourth, gain, *weights)
    peer = lax.ppermute(full, "dp", xor_pairs(count, 1))
    low = jax.ShapeDtypeStruct((2 * half, width + 2 * units), jnp.bfloat16)
    own, away = pl.pallas_call(
        functools.partial(side_kernel, width),
        out_shape=(low, low),
        in_specs=[VMEM] * 2,
        out_specs=[VMEM] * 2,
        compiler_params=pltpu.CompilerParams(vmem_limit_bytes=4 << 20),
    )(full, peer)
    scatter = masks[::-1]
    for step, mask in enumerate(scatter):
        came = lax.ppermute(send, "dp", xor_pairs(count, mask))
        if step + 1 < len(scatter):
            part = keep + came.astype(jnp.float32)
            half = part.shape[0] // 2
            send, keep = part[half:].astype(jnp.bfloat16), part[:half]
    far = lax.ppermute(away, "mirror", xor_pairs(mirrors, 1))
    mid = width // 2
    grad_first, grad_second = pl.pallas_call(
        functools.partial(outer_kernel, 8),
        out_shape=(
            jax.ShapeDtypeStruct((mid, units), jnp.bfloat16),
            jax.ShapeDtypeStruct((units, mid), jnp.bfloat16),
        ),
        in_specs=[VMEM] * 2,
        out_specs=[pl.BlockSpec(memory_space=pl.ANY)] * 2,
        scratch_shapes=[
            pltpu.VMEM((2 * far.shape[0], far.shape[1]), jnp.bfloat16),
            pltpu.VMEM((mid, units), jnp.bfloat16),
            pltpu.VMEM((units, mid), jnp.bfloat16),
            pltpu.SemaphoreType.DMA((2, 8)),
        ],
        compiler_params=pltpu.CompilerParams(vmem_limit_bytes=max(6 << 20, 24 * far.size)),
        cost_estimate=pl.CostEstimate(flops=0, bytes_accessed=8 * mid * units, transcendentals=0),
    )(own, far)
    part, grad_first, grad_second = lax.optimization_barrier((part, grad_first, grad_second))
    fwd_out, bwd_out = pl.pallas_call(
        functools.partial(tail_kernel, rows),
        out_shape=(jax.ShapeDtypeStruct((rows, width), jnp.bfloat16),) * 2,
        in_specs=[VMEM] * 6,
        out_specs=[VMEM] * 2,
        compiler_params=pltpu.CompilerParams(vmem_limit_bytes=max(4 << 20, 40 * rows * width * 4)),
    )(part, came, gain, pair, nhat, rstd)
    return (fwd_out[None, None], bwd_out[None, None], grad_first[None], grad_second[None])


def solution(mesh):
    in_specs = (
        P("section", "mirror", "dp", None),
        P("section", "mirror", "dp", None),
        P("section", "mirror", "dp", None),
        P("section", None),
        P("section", None, "dp"),
        P("section", "dp", None),
    )
    out_specs = (
        P("section", "mirror", "dp", None),
        P("section", "mirror", "dp", None),
        P("section", "mirror", "dp"),
        P("section", "dp", "mirror"),
    )
    return jax.shard_map(
        on_device, mesh=mesh, in_specs=in_specs, out_specs=out_specs, check_vma=False
    )
```

```python
import functools

import jax
import jax.numpy as jnp
from jax import lax
from jax.experimental import pallas as pl
from jax.experimental.pallas import tpu as pltpu
from jax.sharding import PartitionSpec as P

AXES = ("section", "mirror", "dp")
VMEM = pl.BlockSpec(memory_space=pltpu.VMEM)


def xor_pairs(count, mask):
    return [(source, source ^ mask) for source in range(count)]


def relay_pairs(sections, mirrors, count, mask, sign):
    pairs = []
    for section in range(sections):
        for mirror in range(mirrors):
            step = sign if mirror == 0 else -sign
            for dp in range(count):
                source = (section * mirrors + mirror) * count + dp
                target = ((section + step) % sections * mirrors + mirror) * count + (dp ^ mask)
                pairs.append((source, target))
    return sorted(pairs)


def norm_rows(x):
    centre = x - jnp.mean(x, axis=-1, keepdims=True)
    rstd = lax.rsqrt(jnp.mean(centre * centre, axis=-1, keepdims=True) + 1e-05)
    return (centre * rstd, rstd)


def gelu_pair(h):
    coeff = 0.7978845608028654
    inner = coeff * (h + 0.044715 * h * h * h)
    tanh_val = jnp.tanh(inner)
    value = 0.5 * h * (1.0 + tanh_val)
    slope = 0.5 * (1.0 + tanh_val) + 0.5 * h * (1.0 - tanh_val * tanh_val) * coeff * (
        1.0 + 3.0 * 0.044715 * h * h
    )
    return (value, slope)


def dot(left, right, contract):
    return lax.dot_general(left, right, ((contract[:1], contract[1:]), ((), ())), preferred_element_type=jnp.float32)


def spread(ref, scratch, count):
    scratch[...] = ref[...].astype(jnp.float32)
    many = ref.shape[0] // count
    return jnp.concatenate([scratch[pl.ds(k, count, stride=many), :] for k in range(many)], axis=1)


def of_array(ref, array):
    if len(ref.shape) == 3:
        return ref[array].astype(jnp.float32)
    rows = ref.shape[0] // 3
    return ref[array * rows : (array + 1) * rows].astype(jnp.float32)


def block_kernel(rows, outer, fourth, gain, w_in, w_out_t, tall, send, keep, full, leaving, *scratch):
    count, width = keep.shape
    units = w_in.shape[1]
    f32, bf16 = jnp.float32, jnp.bfloat16

    last = spread(fourth, scratch[0], 3 * rows) if scratch else fourth

    def joined(*arrays):
        return jnp.concatenate([of_array(piece, array) for array in arrays for piece in (outer, last)], axis=0)

    cotan = joined(1).astype(bf16)
    d_acted = dot(cotan, w_out_t[...], (1, 0))
    nhat, _ = norm_rows(joined(0, 2))
    normed = (nhat * gain[...]).astype(bf16)
    hidden = dot(normed, w_in[...], (1, 0))
    value, slope = gelu_pair(hidden)
    d_hidden = d_acted * slope[count:]
    leaving[...] = jnp.zeros_like(leaving)
    for slot in range(count // rows):
        source = slice(slot * rows, (slot + 1) * rows)
        leaving[2 * slot * rows : (2 * slot + 1) * rows, :units] = value[source]
        leaving[(2 * slot + 1) * rows : (2 * slot + 2) * rows, units:] = d_hidden[source]
    part = dot(leaving[...].astype(bf16), tall[...], (1, 0))
    send[...] = part[count:].astype(bf16)
    keep[...] = part[:count]
    full[:, :width] = (nhat[count:] * gain[...]).astype(bf16)
    full[:, width : 2 * width] = cotan
    low = units // 2
    value, d_hidden = value[count:].astype(bf16), d_hidden.astype(bf16)
    for side in range(2):
        start = 2 * width + 2 * side * low
        full[:, start : start + low] = value[:, side * low : (side + 1) * low]
        full[:, start + low : start + 2 * low] = d_hidden[:, side * low : (side + 1) * low]


def row_kernel(stash, nhat_out, rstd_out):
    nhat, rstd = norm_rows(stash[...].astype(jnp.float32))
    nhat_out[...] = nhat
    rstd_out[...] = jnp.broadcast_to(rstd, rstd_out.shape)


def stack_kernel(rows, pair, stash, held, *scratch):
    if not scratch:
        held[: 2 * rows] = pair[...]
        held[2 * rows :] = stash[...]
        return
    step, many = held.shape[1], pair.shape[1] // held.shape[1]
    values = jnp.concatenate([pair[...].astype(jnp.float32), stash[...].astype(jnp.float32)], axis=0)
    for row in range(3 * rows):
        for k in range(many):
            scratch[0][many * row + k : many * row + k + 1] = values[row : row + 1, k * step : (k + 1) * step]
    held[...] = scratch[0][...].astype(held.dtype)


def merge_kernel(held, other, merged):
    for array in range(3):
        pieces = [of_array(ref, array) for ref in (held, other)]
        merged[array] = jnp.concatenate(pieces, axis=0).astype(merged.dtype)


def three_kernel(rows, held, second, third, merged, *scratch):
    refs = held, second, third
    if scratch:
        refs = [spread(ref, scratch[0].at[i], 3 * rows) for i, ref in enumerate(refs)]
    for array in range(3):
        pieces = [of_array(ref, array) for ref in refs]
        merged[array] = jnp.concatenate(pieces, axis=0).astype(merged.dtype)


def side_kernel(width, full, peer, own, away):
    count, low, mid = full.shape[0], own.shape[1] - width, width // 2
    upper = lax.axis_index("mirror") == 0
    for ref in (own, away):
        ref[:count, width:] = full[:, 2 * width : 2 * width + low]
        ref[count:, width:] = peer[:, 2 * width + low :]
    for source, target in ((full, slice(0, count)), (peer, slice(count, 2 * count))):

        @pl.when(upper)
        def _(source=source, target=target):
            own[target, :mid] = source[:, :mid]
            own[target, mid:width] = source[:, width : width + mid]
            away[target, :mid] = source[:, mid:width]
            away[target, mid:width] = source[:, width + mid : 2 * width]

        @pl.when(jnp.logical_not(upper))
        def _(source=source, target=target):
            own[target, :mid] = source[:, mid:width]
            own[target, mid:width] = source[:, width + mid : 2 * width]
            away[target, :mid] = source[:, :mid]
            away[target, mid:width] = source[:, width : width + mid]


def load_kernel(chunks, source, target, sems):
    step = source.shape[0] // chunks
    copies = [
        pltpu.make_async_copy(source.at[pl.ds(i * step, step)], target.at[pl.ds(i * step, step)], sems.at[i])
        for i in range(chunks)
    ]
    for copy in copies:
        copy.start()
    for copy in copies:
        copy.wait()


def loaded(weights, chunks):
    size = weights.size * weights.dtype.itemsize
    return pl.pallas_call(
        functools.partial(load_kernel, chunks),
        out_shape=jax.ShapeDtypeStruct(weights.shape, weights.dtype),
        in_specs=[pl.BlockSpec(memory_space=pl.ANY)],
        out_specs=VMEM,
        scratch_shapes=[pltpu.SemaphoreType.DMA((chunks,))],
        compiler_params=pltpu.CompilerParams(vmem_limit_bytes=max(4 << 20, 2 * size)),
        cost_estimate=pl.CostEstimate(flops=0, bytes_accessed=3 * size, transcendentals=0),
    )(weights)


def prepare_kernel(in_own, in_peer, out_own, out_peer, w_in, w_out_t, tall):
    low = in_own.shape[1]
    w_in[:, :low] = in_own[...]
    w_in[:, low:] = in_peer[...]
    w_out_t[:, :low] = out_own[...].T
    w_out_t[:, low:] = out_peer[...].T
    tall[:low] = out_own[...]
    tall[low : 2 * low] = out_peer[...]
    tall[2 * low : 3 * low] = in_own[...].T
    tall[3 * low :] = in_peer[...].T


def prepared(in_own, in_peer, out_own, out_peer):
    width, low = in_own.shape
    size = in_own.size * in_own.dtype.itemsize
    return pl.pallas_call(
        prepare_kernel,
        out_shape=(
            jax.ShapeDtypeStruct((width, 2 * low), in_own.dtype),
            jax.ShapeDtypeStruct((width, 2 * low), in_own.dtype),
            jax.ShapeDtypeStruct((4 * low, width), in_own.dtype),
        ),
        in_specs=[VMEM] * 4,
        out_specs=[VMEM] * 3,
        compiler_params=pltpu.CompilerParams(vmem_limit_bytes=max(4 << 20, 4 * size)),
        cost_estimate=pl.CostEstimate(flops=0, bytes_accessed=6 * size, transcendentals=0),
    )(in_own, in_peer, out_own, out_peer)


def outer_kernel(chunks, own, far, first_out, second_out, pair, first, second, sems):
    rows, (mid, units) = own.shape[0], first.shape
    pair[:rows] = own[...]
    pair[rows:] = far[...]
    value = pair[:, 2 * mid : 2 * mid + units]
    d_hidden = pair[:, 2 * mid + units :]
    copies = []
    step = mid // chunks
    for i in range(chunks):
        part = slice(i * step, (i + 1) * step)
        first[part] = dot(pair[:, part], d_hidden, (0, 0)).astype(first.dtype)
        copies.append(pltpu.make_async_copy(first.at[part], first_out.at[part], sems.at[0, i]))
        copies[-1].start()
    for i in range(chunks):
        part = slice(i * step, (i + 1) * step)
        second[:, part] = dot(value, pair[:, mid + i * step : mid + (i + 1) * step], (0, 0)).astype(second.dtype)
        copies.append(pltpu.make_async_copy(second.at[:, part], second_out.at[:, part], sems.at[1, i]))
        copies[-1].start()
    for copy in copies:
        copy.wait()


def tail_kernel(rows, part, came, gain, pair, nhat_in, rstd, fwd_out, bwd_out):
    f32 = jnp.float32
    branch = part[:rows] + came[:rows].astype(f32)
    fwd_out[...] = (pair[:rows].astype(f32) + branch).astype(fwd_out.dtype)
    scaled = (part[rows : 2 * rows] + came[rows:].astype(f32)) * gain[...]
    nhat = nhat_in[...]
    d_input = rstd[:, :1] * (
        scaled
        - jnp.mean(scaled, axis=-1, keepdims=True)
        - nhat * jnp.mean(scaled * nhat, axis=-1, keepdims=True)
    )
    bwd_out[...] = (pair[rows:].astype(f32) + d_input).astype(bwd_out.dtype)


def on_device(sent_fwd, sent_bwd, stash, gain, w_in, w_out):
    sections, mirrors = lax.axis_size("section"), lax.axis_size("mirror")
    count = lax.axis_size("dp")
    bits = count.bit_length() - 1
    masks = [(1 << bit) | 1 for bit in range(bits - 1, 0, -1)]
    rows, width = sent_fwd.shape[2], sent_fwd.shape[3]
    units = w_in.shape[2]
    onward, back = [relay_pairs(sections, mirrors, count, 0, sign) for sign in (1, -1)]
    if onward == back:
        pair = jnp.concatenate([sent_fwd[0, 0], sent_bwd[0, 0]], axis=0)
        pair = lax.ppermute(pair, AXES, onward)
    else:
        fwd_in = lax.ppermute(sent_fwd[0, 0], AXES, onward)
        bwd_in = lax.ppermute(sent_bwd[0, 0], AXES, back)
        pair = jnp.concatenate([fwd_in, bwd_in], axis=0)
    nhat, rstd = pl.pallas_call(
        row_kernel,
        out_shape=(
            jax.ShapeDtypeStruct((rows, width), jnp.float32),
            jax.ShapeDtypeStruct((rows, 128), jnp.float32),
        ),
        in_specs=[VMEM],
        out_specs=[VMEM] * 2,
        compiler_params=pltpu.CompilerParams(vmem_limit_bytes=max(4 << 20, 40 * rows * width * 4)),
    )(stash[0, 0])
    peer_first, peer_second = [lax.ppermute(source, "dp", xor_pairs(count, 1)) for source in (w_in[0], w_out[0])]
    w_first = loaded(w_in[0], 4)
    pair, w_first = lax.optimization_barrier((pair, w_first))
    w_second = loaded(w_out[0], 4)
    packed = len(masks) == 2 and width % 1024 == 0
    flat = (3 * rows * (width // 128), 128) if packed else (3 * rows, width)
    pieces = [pltpu.VMEM(flat, jnp.float32)] if packed else []
    held = pl.pallas_call(
        functools.partial(stack_kernel, rows),
        out_shape=jax.ShapeDtypeStruct(flat, jnp.bfloat16),
        in_specs=[VMEM] * 2,
        out_specs=VMEM,
        scratch_shapes=pieces,
        compiler_params=pltpu.CompilerParams(vmem_limit_bytes=max(4 << 20, 64 * rows * width)),
        cost_estimate=pl.CostEstimate(flops=20 * 10**9, bytes_accessed=10**5, transcendentals=0),
    )(pair, stash[0, 0])
    slots = rows

    def from_peer(value, mask):
        return lax.ppermute(value, "dp", xor_pairs(count, mask))

    for mask in masks[:-2]:
        other = from_peer(held, mask)
        slots *= 2
        held = pl.pallas_call(
            merge_kernel,
            out_shape=jax.ShapeDtypeStruct((3, slots, width), jnp.bfloat16),
            in_specs=[VMEM] * 2,
            out_specs=VMEM,
            compiler_params=pltpu.CompilerParams(vmem_limit_bytes=max(4 << 20, 48 * slots * width)),
        )(held, other)
    second = from_peer(held, masks[-2])
    third = from_peer(held, masks[-1])
    second, w_second = lax.optimization_barrier((second, w_second))
    fourth = from_peer(second, masks[-1])
    weights = prepared(w_first, peer_first, w_second, peer_second)
    fourth, *weights = lax.optimization_barrier((fourth, *weights))
    slots *= 2
    outer = pl.pallas_call(
        functools.partial(three_kernel, rows),
        out_shape=jax.ShapeDtypeStruct((3, slots // 2 * 3, width), jnp.bfloat16),
        in_specs=[VMEM] * 3,
        out_specs=VMEM,
        scratch_shapes=[pltpu.VMEM((3,) + flat, jnp.float32)] if packed else [],
        compiler_params=pltpu.CompilerParams(vmem_limit_bytes=max(4 << 20, 128 * slots * width)),
        cost_estimate=pl.CostEstimate(flops=10 * 10**9, bytes_accessed=10**5, transcendentals=0),
    )(held, second, third)
    half = 2 * slots
    limit = pltpu.CompilerParams(vmem_limit_bytes=max(8 << 20, 40 * half * width * 4))
    send, keep, full = pl.pallas_call(
        functools.partial(block_kernel, rows),
        out_shape=(
            jax.ShapeDtypeStruct((half, width), jnp.bfloat16),
            jax.ShapeDtypeStruct((half, width), jnp.float32),
            jax.ShapeDtypeStruct((half, 2 * width + 4 * units), jnp.bfloat16),
        ),
        in_specs=[VMEM] * 6,
        out_specs=[VMEM] * 3,
        scratch_shapes=[pltpu.VMEM((2 * half, 4 * units), jnp.float32)] + pieces,
        compiler_params=limit,
    )(outer, fourth, gain, *weights)
    peer = lax.ppermute(full, "dp", xor_pairs(count, 1))
    low = jax.ShapeDtypeStruct((2 * half, width + 2 * units), jnp.bfloat16)
    own, away = pl.pallas_call(
        functools.partial(side_kernel, width),
        out_shape=(low, low),
        in_specs=[VMEM] * 2,
        out_specs=[VMEM] * 2,
        compiler_params=pltpu.CompilerParams(vmem_limit_bytes=4 << 20),
    )(full, peer)
    scatter = masks[::-1]
    for step, mask in enumerate(scatter):
        came = lax.ppermute(send, "dp", xor_pairs(count, mask))
        if step + 1 < len(scatter):
            part = keep + came.astype(jnp.float32)
            if step == 0:
                part, nhat, rstd = lax.optimization_barrier((part, nhat, rstd))
            half = part.shape[0] // 2
            send, keep = part[half:].astype(jnp.bfloat16), part[:half]
    far = lax.ppermute(away, "mirror", xor_pairs(mirrors, 1))
    mid = width // 2
    grad_first, grad_second = pl.pallas_call(
        functools.partial(outer_kernel, 8),
        out_shape=(
            jax.ShapeDtypeStruct((mid, units), jnp.bfloat16),
            jax.ShapeDtypeStruct((units, mid), jnp.bfloat16),
        ),
        in_specs=[VMEM] * 2,
        out_specs=[pl.BlockSpec(memory_space=pl.ANY)] * 2,
        scratch_shapes=[
            pltpu.VMEM((2 * far.shape[0], far.shape[1]), jnp.bfloat16),
            pltpu.VMEM((mid, units), jnp.bfloat16),
            pltpu.VMEM((units, mid), jnp.bfloat16),
            pltpu.SemaphoreType.DMA((2, 8)),
        ],
        compiler_params=pltpu.CompilerParams(vmem_limit_bytes=max(6 << 20, 24 * far.size)),
        cost_estimate=pl.CostEstimate(flops=0, bytes_accessed=8 * mid * units, transcendentals=0),
    )(own, far)
    part, grad_first, grad_second = lax.optimization_barrier((part, grad_first, grad_second))
    fwd_out, bwd_out = pl.pallas_call(
        functools.partial(tail_kernel, rows),
        out_shape=(jax.ShapeDtypeStruct((rows, width), jnp.bfloat16),) * 2,
        in_specs=[VMEM] * 6,
        out_specs=[VMEM] * 2,
        compiler_params=pltpu.CompilerParams(vmem_limit_bytes=max(4 << 20, 40 * rows * width * 4)),
    )(part, came, gain, pair, nhat, rstd)
    return (fwd_out[None, None], bwd_out[None, None], grad_first[None], grad_second[None])


def solution(mesh):
    in_specs = (
        P("section", "mirror", "dp", None),
        P("section", "mirror", "dp", None),
        P("section", "mirror", "dp", None),
        P("section", None),
        P("section", None, "dp"),
        P("section", "dp", None),
    )
    out_specs = (
        P("section", "mirror", "dp", None),
        P("section", "mirror", "dp", None),
        P("section", "mirror", "dp"),
        P("section", "dp", "mirror"),
    )
    return jax.shard_map(
        on_device, mesh=mesh, in_specs=in_specs, out_specs=out_specs, check_vma=False
    )
```

```python
import functools

import jax
import jax.numpy as jnp
from jax import lax
from jax.experimental import pallas as pl
from jax.experimental.pallas import tpu as pltpu
from jax.sharding import PartitionSpec as P

AXES = ("section", "mirror", "dp")
VMEM = pl.BlockSpec(memory_space=pltpu.VMEM)


def xor_pairs(count, mask):
    return [(source, source ^ mask) for source in range(count)]


def relay_pairs(sections, mirrors, count, mask, sign):
    pairs = []
    for section in range(sections):
        for mirror in range(mirrors):
            step = sign if mirror == 0 else -sign
            for dp in range(count):
                source = (section * mirrors + mirror) * count + dp
                target = ((section + step) % sections * mirrors + mirror) * count + (dp ^ mask)
                pairs.append((source, target))
    return sorted(pairs)


def norm_rows(x):
    centre = x - jnp.mean(x, axis=-1, keepdims=True)
    rstd = lax.rsqrt(jnp.mean(centre * centre, axis=-1, keepdims=True) + 1e-05)
    return (centre * rstd, rstd)


def gelu_pair(h):
    coeff = 0.7978845608028654
    inner = coeff * (h + 0.044715 * h * h * h)
    tanh_val = jnp.tanh(inner)
    value = 0.5 * h * (1.0 + tanh_val)
    slope = 0.5 * (1.0 + tanh_val) + 0.5 * h * (1.0 - tanh_val * tanh_val) * coeff * (
        1.0 + 3.0 * 0.044715 * h * h
    )
    return (value, slope)


def dot(left, right, contract):
    return lax.dot_general(left, right, ((contract[:1], contract[1:]), ((), ())), preferred_element_type=jnp.float32)


def spread(ref, scratch, count):
    scratch[...] = ref[...].astype(jnp.float32)
    many = ref.shape[0] // count
    return jnp.concatenate([scratch[pl.ds(k, count, stride=many), :] for k in range(many)], axis=1)


def of_array(ref, array):
    if len(ref.shape) == 3:
        return ref[array].astype(jnp.float32)
    rows = ref.shape[0] // 3
    return ref[array * rows : (array + 1) * rows].astype(jnp.float32)


def block_kernel(rows, outer, fourth, gain, w_in, w_out_t, tall, send, keep, full, leaving, *scratch):
    count, width = keep.shape
    units = w_in.shape[1]
    f32, bf16 = jnp.float32, jnp.bfloat16

    last = spread(fourth, scratch[0], 3 * rows) if scratch else fourth

    def joined(*arrays):
        return jnp.concatenate([of_array(piece, array) for array in arrays for piece in (outer, last)], axis=0)

    cotan = joined(1).astype(bf16)
    d_acted = dot(cotan, w_out_t[...], (1, 0))
    nhat, _ = norm_rows(joined(0, 2))
    normed = (nhat * gain[...]).astype(bf16)
    hidden = dot(normed, w_in[...], (1, 0))
    value, slope = gelu_pair(hidden)
    d_hidden = d_acted * slope[count:]
    leaving[...] = jnp.zeros_like(leaving)
    for slot in range(count // rows):
        source = slice(slot * rows, (slot + 1) * rows)
        leaving[2 * slot * rows : (2 * slot + 1) * rows, :units] = value[source]
        leaving[(2 * slot + 1) * rows : (2 * slot + 2) * rows, units:] = d_hidden[source]
    part = dot(leaving[...].astype(bf16), tall[...], (1, 0))
    send[...] = part[count:].astype(bf16)
    keep[...] = part[:count]
    full[:, :width] = (nhat[count:] * gain[...]).astype(bf16)
    full[:, width : 2 * width] = cotan
    low = units // 2
    value, d_hidden = value[count:].astype(bf16), d_hidden.astype(bf16)
    for side in range(2):
        start = 2 * width + 2 * side * low
        full[:, start : start + low] = value[:, side * low : (side + 1) * low]
        full[:, start + low : start + 2 * low] = d_hidden[:, side * low : (side + 1) * low]


def row_kernel(stash, nhat_out, rstd_out):
    nhat, rstd = norm_rows(stash[...].astype(jnp.float32))
    nhat_out[...] = nhat
    rstd_out[...] = jnp.broadcast_to(rstd, rstd_out.shape)


def stack_kernel(rows, pair, stash, held, *scratch):
    if not scratch:
        held[: 2 * rows] = pair[...]
        held[2 * rows :] = stash[...]
        return
    step, many = held.shape[1], pair.shape[1] // held.shape[1]
    values = jnp.concatenate([pair[...].astype(jnp.float32), stash[...].astype(jnp.float32)], axis=0)
    for row in range(3 * rows):
        for k in range(many):
            scratch[0][many * row + k : many * row + k + 1] = values[row : row + 1, k * step : (k + 1) * step]
    held[...] = scratch[0][...].astype(held.dtype)


def merge_kernel(held, other, merged):
    for array in range(3):
        pieces = [of_array(ref, array) for ref in (held, other)]
        merged[array] = jnp.concatenate(pieces, axis=0).astype(merged.dtype)


def three_kernel(rows, held, second, third, merged, *scratch):
    refs = held, second, third
    if scratch:
        refs = [spread(ref, scratch[0].at[i], 3 * rows) for i, ref in enumerate(refs)]
    for array in range(3):
        pieces = [of_array(ref, array) for ref in refs]
        merged[array] = jnp.concatenate(pieces, axis=0).astype(merged.dtype)


def side_kernel(width, full, peer, own, away):
    count, low, mid = full.shape[0], own.shape[1] - width, width // 2
    upper = lax.axis_index("mirror") == 0
    for ref in (own, away):
        ref[:count, width:] = full[:, 2 * width : 2 * width + low]
        ref[count:, width:] = peer[:, 2 * width + low :]
    for source, target in ((full, slice(0, count)), (peer, slice(count, 2 * count))):

        @pl.when(upper)
        def _(source=source, target=target):
            own[target, :mid] = source[:, :mid]
            own[target, mid:width] = source[:, width : width + mid]
            away[target, :mid] = source[:, mid:width]
            away[target, mid:width] = source[:, width + mid : 2 * width]

        @pl.when(jnp.logical_not(upper))
        def _(source=source, target=target):
            own[target, :mid] = source[:, mid:width]
            own[target, mid:width] = source[:, width + mid : 2 * width]
            away[target, :mid] = source[:, :mid]
            away[target, mid:width] = source[:, width : width + mid]


def load_kernel(chunks, source, target, sems):
    step = source.shape[0] // chunks
    copies = [
        pltpu.make_async_copy(source.at[pl.ds(i * step, step)], target.at[pl.ds(i * step, step)], sems.at[i])
        for i in range(chunks)
    ]
    for copy in copies:
        copy.start()
    for copy in copies:
        copy.wait()


def loaded(weights, chunks):
    size = weights.size * weights.dtype.itemsize
    return pl.pallas_call(
        functools.partial(load_kernel, chunks),
        out_shape=jax.ShapeDtypeStruct(weights.shape, weights.dtype),
        in_specs=[pl.BlockSpec(memory_space=pl.ANY)],
        out_specs=VMEM,
        scratch_shapes=[pltpu.SemaphoreType.DMA((chunks,))],
        compiler_params=pltpu.CompilerParams(vmem_limit_bytes=max(4 << 20, 2 * size)),
        cost_estimate=pl.CostEstimate(flops=0, bytes_accessed=3 * size, transcendentals=0),
    )(weights)


def prepare_kernel(in_own, in_peer, out_own, out_peer, w_in, w_out_t, tall):
    low = in_own.shape[1]
    w_in[:, :low] = in_own[...]
    w_in[:, low:] = in_peer[...]
    w_out_t[:, :low] = out_own[...].T
    w_out_t[:, low:] = out_peer[...].T
    tall[:low] = out_own[...]
    tall[low : 2 * low] = out_peer[...]
    tall[2 * low : 3 * low] = in_own[...].T
    tall[3 * low :] = in_peer[...].T


def prepared(in_own, in_peer, out_own, out_peer):
    width, low = in_own.shape
    size = in_own.size * in_own.dtype.itemsize
    return pl.pallas_call(
        prepare_kernel,
        out_shape=(
            jax.ShapeDtypeStruct((width, 2 * low), in_own.dtype),
            jax.ShapeDtypeStruct((width, 2 * low), in_own.dtype),
            jax.ShapeDtypeStruct((4 * low, width), in_own.dtype),
        ),
        in_specs=[VMEM] * 4,
        out_specs=[VMEM] * 3,
        compiler_params=pltpu.CompilerParams(vmem_limit_bytes=max(4 << 20, 4 * size)),
        cost_estimate=pl.CostEstimate(flops=0, bytes_accessed=6 * size, transcendentals=0),
    )(in_own, in_peer, out_own, out_peer)


def outer_kernel(chunks, own, far, first_out, second_out, pair, first, second, sems):
    rows, (mid, units) = own.shape[0], first.shape
    pair[:rows] = own[...]
    pair[rows:] = far[...]
    value = pair[:, 2 * mid : 2 * mid + units]
    d_hidden = pair[:, 2 * mid + units :]
    copies = []
    step = mid // chunks
    for i in range(chunks):
        part = slice(i * step, (i + 1) * step)
        first[part] = dot(pair[:, part], d_hidden, (0, 0)).astype(first.dtype)
        copies.append(pltpu.make_async_copy(first.at[part], first_out.at[part], sems.at[0, i]))
        copies[-1].start()
    for i in range(chunks):
        part = slice(i * step, (i + 1) * step)
        second[:, part] = dot(value, pair[:, mid + i * step : mid + (i + 1) * step], (0, 0)).astype(second.dtype)
        copies.append(pltpu.make_async_copy(second.at[:, part], second_out.at[:, part], sems.at[1, i]))
        copies[-1].start()
    for copy in copies:
        copy.wait()


def tail_kernel(rows, part, came, gain, pair, nhat_in, rstd, fwd_out, bwd_out):
    f32 = jnp.float32
    branch = part[:rows] + came[:rows].astype(f32)
    fwd_out[...] = (pair[:rows].astype(f32) + branch).astype(fwd_out.dtype)
    scaled = (part[rows : 2 * rows] + came[rows:].astype(f32)) * gain[...]
    nhat = nhat_in[...]
    d_input = rstd[:, :1] * (
        scaled
        - jnp.mean(scaled, axis=-1, keepdims=True)
        - nhat * jnp.mean(scaled * nhat, axis=-1, keepdims=True)
    )
    bwd_out[...] = (pair[rows:].astype(f32) + d_input).astype(bwd_out.dtype)


def on_device(sent_fwd, sent_bwd, stash, gain, w_in, w_out):
    sections, mirrors = lax.axis_size("section"), lax.axis_size("mirror")
    count = lax.axis_size("dp")
    bits = count.bit_length() - 1
    masks = [(1 << bit) | 1 for bit in range(bits - 1, 0, -1)]
    rows, width = sent_fwd.shape[2], sent_fwd.shape[3]
    units = w_in.shape[2]
    onward, back = [relay_pairs(sections, mirrors, count, 0, sign) for sign in (1, -1)]
    if onward == back:
        pair = jnp.concatenate([sent_fwd[0, 0], sent_bwd[0, 0]], axis=0)
        pair = lax.ppermute(pair, AXES, onward)
    else:
        fwd_in = lax.ppermute(sent_fwd[0, 0], AXES, onward)
        bwd_in = lax.ppermute(sent_bwd[0, 0], AXES, back)
        pair = jnp.concatenate([fwd_in, bwd_in], axis=0)
    nhat, rstd = pl.pallas_call(
        row_kernel,
        out_shape=(
            jax.ShapeDtypeStruct((rows, width), jnp.float32),
            jax.ShapeDtypeStruct((rows, 128), jnp.float32),
        ),
        in_specs=[VMEM],
        out_specs=[VMEM] * 2,
        compiler_params=pltpu.CompilerParams(vmem_limit_bytes=max(4 << 20, 40 * rows * width * 4)),
    )(stash[0, 0])
    peer_first, peer_second = [lax.ppermute(source, "dp", xor_pairs(count, 1)) for source in (w_in[0], w_out[0])]
    w_first = loaded(w_in[0], 4)
    pair, w_first = lax.optimization_barrier((pair, w_first))
    w_second = loaded(w_out[0], 4)
    packed = len(masks) == 2 and width % 1024 == 0
    flat = (3 * rows * (width // 128), 128) if packed else (3 * rows, width)
    pieces = [pltpu.VMEM(flat, jnp.float32)] if packed else []
    held = pl.pallas_call(
        functools.partial(stack_kernel, rows),
        out_shape=jax.ShapeDtypeStruct(flat, jnp.bfloat16),
        in_specs=[VMEM] * 2,
        out_specs=VMEM,
        scratch_shapes=pieces,
        compiler_params=pltpu.CompilerParams(vmem_limit_bytes=max(4 << 20, 64 * rows * width)),
        cost_estimate=pl.CostEstimate(flops=20 * 10**9, bytes_accessed=10**5, transcendentals=0),
    )(pair, stash[0, 0])
    slots = rows

    def from_peer(value, mask):
        return lax.ppermute(value, "dp", xor_pairs(count, mask))

    for mask in masks[:-2]:
        other = from_peer(held, mask)
        slots *= 2
        held = pl.pallas_call(
            merge_kernel,
            out_shape=jax.ShapeDtypeStruct((3, slots, width), jnp.bfloat16),
            in_specs=[VMEM] * 2,
            out_specs=VMEM,
            compiler_params=pltpu.CompilerParams(vmem_limit_bytes=max(4 << 20, 48 * slots * width)),
        )(held, other)
    second = from_peer(held, masks[-2])
    third = from_peer(held, masks[-1])
    second, nhat, rstd = lax.optimization_barrier((second, nhat, rstd))
    fourth = from_peer(second, masks[-1])
    weights = prepared(w_first, peer_first, w_second, peer_second)
    fourth, *weights = lax.optimization_barrier((fourth, *weights))
    slots *= 2
    outer = pl.pallas_call(
        functools.partial(three_kernel, rows),
        out_shape=jax.ShapeDtypeStruct((3, slots // 2 * 3, width), jnp.bfloat16),
        in_specs=[VMEM] * 3,
        out_specs=VMEM,
        scratch_shapes=[pltpu.VMEM((3,) + flat, jnp.float32)] if packed else [],
        compiler_params=pltpu.CompilerParams(vmem_limit_bytes=max(4 << 20, 128 * slots * width)),
        cost_estimate=pl.CostEstimate(flops=10 * 10**9, bytes_accessed=10**5, transcendentals=0),
    )(held, second, third)
    half = 2 * slots
    limit = pltpu.CompilerParams(vmem_limit_bytes=max(8 << 20, 40 * half * width * 4))
    send, keep, full = pl.pallas_call(
        functools.partial(block_kernel, rows),
        out_shape=(
            jax.ShapeDtypeStruct((half, width), jnp.bfloat16),
            jax.ShapeDtypeStruct((half, width), jnp.float32),
            jax.ShapeDtypeStruct((half, 2 * width + 4 * units), jnp.bfloat16),
        ),
        in_specs=[VMEM] * 6,
        out_specs=[VMEM] * 3,
        scratch_shapes=[pltpu.VMEM((2 * half, 4 * units), jnp.float32)] + pieces,
        compiler_params=limit,
    )(outer, fourth, gain, *weights)
    peer = lax.ppermute(full, "dp", xor_pairs(count, 1))
    low = jax.ShapeDtypeStruct((2 * half, width + 2 * units), jnp.bfloat16)
    own, away = pl.pallas_call(
        functools.partial(side_kernel, width),
        out_shape=(low, low),
        in_specs=[VMEM] * 2,
        out_specs=[VMEM] * 2,
        compiler_params=pltpu.CompilerParams(vmem_limit_bytes=4 << 20),
    )(full, peer)
    scatter = masks[::-1]
    for step, mask in enumerate(scatter):
        came = lax.ppermute(send, "dp", xor_pairs(count, mask))
        if step + 1 < len(scatter):
            part = keep + came.astype(jnp.float32)
            half = part.shape[0] // 2
            send, keep = part[half:].astype(jnp.bfloat16), part[:half]
    far = lax.ppermute(away, "mirror", xor_pairs(mirrors, 1))
    mid = width // 2
    grad_first, grad_second = pl.pallas_call(
        functools.partial(outer_kernel, 8),
        out_shape=(
            jax.ShapeDtypeStruct((mid, units), jnp.bfloat16),
            jax.ShapeDtypeStruct((units, mid), jnp.bfloat16),
        ),
        in_specs=[VMEM] * 2,
        out_specs=[pl.BlockSpec(memory_space=pl.ANY)] * 2,
        scratch_shapes=[
            pltpu.VMEM((2 * far.shape[0], far.shape[1]), jnp.bfloat16),
            pltpu.VMEM((mid, units), jnp.bfloat16),
            pltpu.VMEM((units, mid), jnp.bfloat16),
            pltpu.SemaphoreType.DMA((2, 8)),
        ],
        compiler_params=pltpu.CompilerParams(vmem_limit_bytes=max(6 << 20, 24 * far.size)),
        cost_estimate=pl.CostEstimate(flops=0, bytes_accessed=8 * mid * units, transcendentals=0),
    )(own, far)
    part, grad_first, grad_second = lax.optimization_barrier((part, grad_first, grad_second))
    fwd_out, bwd_out = pl.pallas_call(
        functools.partial(tail_kernel, rows),
        out_shape=(jax.ShapeDtypeStruct((rows, width), jnp.bfloat16),) * 2,
        in_specs=[VMEM] * 6,
        out_specs=[VMEM] * 2,
        compiler_params=pltpu.CompilerParams(vmem_limit_bytes=max(4 << 20, 40 * rows * width * 4)),
    )(part, came, gain, pair, nhat, rstd)
    return (fwd_out[None, None], bwd_out[None, None], grad_first[None], grad_second[None])


def solution(mesh):
    in_specs = (
        P("section", "mirror", "dp", None),
        P("section", "mirror", "dp", None),
        P("section", "mirror", "dp", None),
        P("section", None),
        P("section", None, "dp"),
        P("section", "dp", None),
    )
    out_specs = (
        P("section", "mirror", "dp", None),
        P("section", "mirror", "dp", None),
        P("section", "mirror", "dp"),
        P("section", "dp", "mirror"),
    )
    return jax.shard_map(
        on_device, mesh=mesh, in_specs=in_specs, out_specs=out_specs, check_vma=False
    )
```

```python
import functools

import jax
import jax.numpy as jnp
from jax import lax
from jax.experimental import pallas as pl
from jax.experimental.pallas import tpu as pltpu
from jax.sharding import PartitionSpec as P

AXES = ("section", "mirror", "dp")
VMEM = pl.BlockSpec(memory_space=pltpu.VMEM)


def xor_pairs(count, mask):
    return [(source, source ^ mask) for source in range(count)]


def relay_pairs(sections, mirrors, count, mask, sign):
    pairs = []
    for section in range(sections):
        for mirror in range(mirrors):
            step = sign if mirror == 0 else -sign
            for dp in range(count):
                source = (section * mirrors + mirror) * count + dp
                target = ((section + step) % sections * mirrors + mirror) * count + (dp ^ mask)
                pairs.append((source, target))
    return sorted(pairs)


def norm_rows(x):
    centre = x - jnp.mean(x, axis=-1, keepdims=True)
    rstd = lax.rsqrt(jnp.mean(centre * centre, axis=-1, keepdims=True) + 1e-05)
    return (centre * rstd, rstd)


def gelu_pair(h):
    coeff = 0.7978845608028654
    inner = coeff * (h + 0.044715 * h * h * h)
    tanh_val = jnp.tanh(inner)
    value = 0.5 * h * (1.0 + tanh_val)
    slope = 0.5 * (1.0 + tanh_val) + 0.5 * h * (1.0 - tanh_val * tanh_val) * coeff * (
        1.0 + 3.0 * 0.044715 * h * h
    )
    return (value, slope)


def dot(left, right, contract):
    return lax.dot_general(left, right, ((contract[:1], contract[1:]), ((), ())), preferred_element_type=jnp.float32)


def spread(ref, scratch, count):
    scratch[...] = ref[...].astype(jnp.float32)
    many = ref.shape[0] // count
    return jnp.concatenate([scratch[pl.ds(k, count, stride=many), :] for k in range(many)], axis=1)


def of_array(ref, array):
    if len(ref.shape) == 3:
        return ref[array].astype(jnp.float32)
    rows = ref.shape[0] // 3
    return ref[array * rows : (array + 1) * rows].astype(jnp.float32)


def block_kernel(rows, outer, fourth, gain, w_in, w_out_t, tall, send, keep, full, leaving, *scratch):
    count, width = keep.shape
    units = w_in.shape[1]
    f32, bf16 = jnp.float32, jnp.bfloat16

    last = spread(fourth, scratch[0], 3 * rows) if scratch else fourth

    def joined(*arrays):
        return jnp.concatenate([of_array(piece, array) for array in arrays for piece in (outer, last)], axis=0)

    cotan = joined(1).astype(bf16)
    d_acted = dot(cotan, w_out_t[...], (1, 0))
    nhat, _ = norm_rows(joined(0, 2))
    normed = (nhat * gain[...]).astype(bf16)
    hidden = dot(normed, w_in[...], (1, 0))
    value, slope = gelu_pair(hidden)
    d_hidden = d_acted * slope[count:]
    leaving[...] = jnp.zeros_like(leaving)
    for slot in range(count // rows):
        source = slice(slot * rows, (slot + 1) * rows)
        leaving[2 * slot * rows : (2 * slot + 1) * rows, :units] = value[source]
        leaving[(2 * slot + 1) * rows : (2 * slot + 2) * rows, units:] = d_hidden[source]
    part = dot(leaving[...].astype(bf16), tall[...], (1, 0))
    send[...] = part[count:].astype(bf16)
    keep[...] = part[:count]
    full[:, :width] = (nhat[count:] * gain[...]).astype(bf16)
    full[:, width : 2 * width] = cotan
    low = units // 2
    value, d_hidden = value[count:].astype(bf16), d_hidden.astype(bf16)
    for side in range(2):
        start = 2 * width + 2 * side * low
        full[:, start : start + low] = value[:, side * low : (side + 1) * low]
        full[:, start + low : start + 2 * low] = d_hidden[:, side * low : (side + 1) * low]


def row_kernel(stash, nhat_out, rstd_out):
    nhat, rstd = norm_rows(stash[...].astype(jnp.float32))
    nhat_out[...] = nhat
    rstd_out[...] = jnp.broadcast_to(rstd, rstd_out.shape)


def stack_kernel(rows, pair, stash, held, *scratch):
    if not scratch:
        held[: 2 * rows] = pair[...]
        held[2 * rows :] = stash[...]
        return
    step, many = held.shape[1], pair.shape[1] // held.shape[1]
    values = jnp.concatenate([pair[...].astype(jnp.float32), stash[...].astype(jnp.float32)], axis=0)
    for row in range(3 * rows):
        for k in range(many):
            scratch[0][many * row + k : many * row + k + 1] = values[row : row + 1, k * step : (k + 1) * step]
    held[...] = scratch[0][...].astype(held.dtype)


def merge_kernel(held, other, merged):
    for array in range(3):
        pieces = [of_array(ref, array) for ref in (held, other)]
        merged[array] = jnp.concatenate(pieces, axis=0).astype(merged.dtype)


def three_kernel(rows, held, second, third, merged, *scratch):
    refs = held, second, third
    if scratch:
        refs = [spread(ref, scratch[0].at[i], 3 * rows) for i, ref in enumerate(refs)]
    for array in range(3):
        pieces = [of_array(ref, array) for ref in refs]
        merged[array] = jnp.concatenate(pieces, axis=0).astype(merged.dtype)


def side_kernel(width, full, peer, own, away):
    count, low, mid = full.shape[0], own.shape[1] - width, width // 2
    upper = lax.axis_index("mirror") == 0
    for ref in (own, away):
        ref[:count, width:] = full[:, 2 * width : 2 * width + low]
        ref[count:, width:] = peer[:, 2 * width + low :]
    for source, target in ((full, slice(0, count)), (peer, slice(count, 2 * count))):

        @pl.when(upper)
        def _(source=source, target=target):
            own[target, :mid] = source[:, :mid]
            own[target, mid:width] = source[:, width : width + mid]
            away[target, :mid] = source[:, mid:width]
            away[target, mid:width] = source[:, width + mid : 2 * width]

        @pl.when(jnp.logical_not(upper))
        def _(source=source, target=target):
            own[target, :mid] = source[:, mid:width]
            own[target, mid:width] = source[:, width + mid : 2 * width]
            away[target, :mid] = source[:, :mid]
            away[target, mid:width] = source[:, width : width + mid]


def load_kernel(chunks, source, target, sems):
    step = source.shape[0] // chunks
    copies = [
        pltpu.make_async_copy(source.at[pl.ds(i * step, step)], target.at[pl.ds(i * step, step)], sems.at[i])
        for i in range(chunks)
    ]
    for copy in copies:
        copy.start()
    for copy in copies:
        copy.wait()


def loaded(weights, chunks):
    size = weights.size * weights.dtype.itemsize
    return pl.pallas_call(
        functools.partial(load_kernel, chunks),
        out_shape=jax.ShapeDtypeStruct(weights.shape, weights.dtype),
        in_specs=[pl.BlockSpec(memory_space=pl.ANY)],
        out_specs=VMEM,
        scratch_shapes=[pltpu.SemaphoreType.DMA((chunks,))],
        compiler_params=pltpu.CompilerParams(vmem_limit_bytes=max(4 << 20, 2 * size)),
        cost_estimate=pl.CostEstimate(flops=0, bytes_accessed=3 * size, transcendentals=0),
    )(weights)


def prepare_kernel(in_own, in_peer, out_own, out_peer, w_in, w_out_t, tall):
    low = in_own.shape[1]
    w_in[:, :low] = in_own[...]
    w_in[:, low:] = in_peer[...]
    w_out_t[:, :low] = out_own[...].T
    w_out_t[:, low:] = out_peer[...].T
    tall[:low] = out_own[...]
    tall[low : 2 * low] = out_peer[...]
    tall[2 * low : 3 * low] = in_own[...].T
    tall[3 * low :] = in_peer[...].T


def prepared(in_own, in_peer, out_own, out_peer):
    width, low = in_own.shape
    size = in_own.size * in_own.dtype.itemsize
    return pl.pallas_call(
        prepare_kernel,
        out_shape=(
            jax.ShapeDtypeStruct((width, 2 * low), in_own.dtype),
            jax.ShapeDtypeStruct((width, 2 * low), in_own.dtype),
            jax.ShapeDtypeStruct((4 * low, width), in_own.dtype),
        ),
        in_specs=[VMEM] * 4,
        out_specs=[VMEM] * 3,
        compiler_params=pltpu.CompilerParams(vmem_limit_bytes=max(4 << 20, 4 * size)),
        cost_estimate=pl.CostEstimate(flops=0, bytes_accessed=6 * size, transcendentals=0),
    )(in_own, in_peer, out_own, out_peer)


def outer_kernel(chunks, own, far, first_out, second_out, pair, first, second, sems):
    rows, (mid, units) = own.shape[0], first.shape
    pair[:rows] = own[...]
    pair[rows:] = far[...]
    value = pair[:, 2 * mid : 2 * mid + units]
    d_hidden = pair[:, 2 * mid + units :]
    copies = []
    step = mid // chunks
    for i in range(chunks):
        part = slice(i * step, (i + 1) * step)
        first[part] = dot(pair[:, part], d_hidden, (0, 0)).astype(first.dtype)
        copies.append(pltpu.make_async_copy(first.at[part], first_out.at[part], sems.at[0, i]))
        copies[-1].start()
    for i in range(chunks):
        part = slice(i * step, (i + 1) * step)
        second[:, part] = dot(value, pair[:, mid + i * step : mid + (i + 1) * step], (0, 0)).astype(second.dtype)
        copies.append(pltpu.make_async_copy(second.at[:, part], second_out.at[:, part], sems.at[1, i]))
        copies[-1].start()
    for copy in copies:
        copy.wait()


def tail_kernel(rows, part, came, gain, pair, nhat_in, rstd, fwd_out, bwd_out):
    f32 = jnp.float32
    branch = part[:rows] + came[:rows].astype(f32)
    fwd_out[...] = (pair[:rows].astype(f32) + branch).astype(fwd_out.dtype)
    scaled = (part[rows : 2 * rows] + came[rows:].astype(f32)) * gain[...]
    nhat = nhat_in[...]
    d_input = rstd[:, :1] * (
        scaled
        - jnp.mean(scaled, axis=-1, keepdims=True)
        - nhat * jnp.mean(scaled * nhat, axis=-1, keepdims=True)
    )
    bwd_out[...] = (pair[rows:].astype(f32) + d_input).astype(bwd_out.dtype)


def on_device(sent_fwd, sent_bwd, stash, gain, w_in, w_out):
    sections, mirrors = lax.axis_size("section"), lax.axis_size("mirror")
    count = lax.axis_size("dp")
    bits = count.bit_length() - 1
    masks = [(1 << bit) | 1 for bit in range(bits - 1, 0, -1)]
    rows, width = sent_fwd.shape[2], sent_fwd.shape[3]
    units = w_in.shape[2]
    onward, back = [relay_pairs(sections, mirrors, count, 0, sign) for sign in (1, -1)]
    if onward == back:
        pair = jnp.concatenate([sent_fwd[0, 0], sent_bwd[0, 0]], axis=0)
        pair = lax.ppermute(pair, AXES, onward)
    else:
        fwd_in = lax.ppermute(sent_fwd[0, 0], AXES, onward)
        bwd_in = lax.ppermute(sent_bwd[0, 0], AXES, back)
        pair = jnp.concatenate([fwd_in, bwd_in], axis=0)
    nhat, rstd = pl.pallas_call(
        row_kernel,
        out_shape=(
            jax.ShapeDtypeStruct((rows, width), jnp.float32),
            jax.ShapeDtypeStruct((rows, 128), jnp.float32),
        ),
        in_specs=[VMEM],
        out_specs=[VMEM] * 2,
        compiler_params=pltpu.CompilerParams(vmem_limit_bytes=max(4 << 20, 40 * rows * width * 4)),
    )(stash[0, 0])
    peer_first, peer_second = [lax.ppermute(source, "dp", xor_pairs(count, 1)) for source in (w_in[0], w_out[0])]
    w_first = loaded(w_in[0], 4)
    pair, w_first = lax.optimization_barrier((pair, w_first))
    w_second = loaded(w_out[0], 4)
    packed = len(masks) == 2 and width % 1024 == 0
    flat = (3 * rows * (width // 128), 128) if packed else (3 * rows, width)
    pieces = [pltpu.VMEM(flat, jnp.float32)] if packed else []
    held = pl.pallas_call(
        functools.partial(stack_kernel, rows),
        out_shape=jax.ShapeDtypeStruct(flat, jnp.bfloat16),
        in_specs=[VMEM] * 2,
        out_specs=VMEM,
        scratch_shapes=pieces,
        compiler_params=pltpu.CompilerParams(vmem_limit_bytes=max(4 << 20, 64 * rows * width)),
        cost_estimate=pl.CostEstimate(flops=20 * 10**9, bytes_accessed=10**5, transcendentals=0),
    )(pair, stash[0, 0])
    slots = rows

    def from_peer(value, mask):
        return lax.ppermute(value, "dp", xor_pairs(count, mask))

    for mask in masks[:-2]:
        other = from_peer(held, mask)
        slots *= 2
        held = pl.pallas_call(
            merge_kernel,
            out_shape=jax.ShapeDtypeStruct((3, slots, width), jnp.bfloat16),
            in_specs=[VMEM] * 2,
            out_specs=VMEM,
            compiler_params=pltpu.CompilerParams(vmem_limit_bytes=max(4 << 20, 48 * slots * width)),
        )(held, other)
    second = from_peer(held, masks[-2])
    third = from_peer(held, masks[-1])
    fourth = from_peer(second, masks[-1])
    weights = prepared(w_first, peer_first, w_second, peer_second)
    fourth, *weights = lax.optimization_barrier((fourth, *weights))
    slots *= 2
    outer = pl.pallas_call(
        functools.partial(three_kernel, rows),
        out_shape=jax.ShapeDtypeStruct((3, slots // 2 * 3, width), jnp.bfloat16),
        in_specs=[VMEM] * 3,
        out_specs=VMEM,
        scratch_shapes=[pltpu.VMEM((3,) + flat, jnp.float32)] if packed else [],
        compiler_params=pltpu.CompilerParams(vmem_limit_bytes=max(4 << 20, 128 * slots * width)),
        cost_estimate=pl.CostEstimate(flops=10 * 10**9, bytes_accessed=10**5, transcendentals=0),
    )(held, second, third)
    half = 2 * slots
    limit = pltpu.CompilerParams(vmem_limit_bytes=max(8 << 20, 40 * half * width * 4))
    send, keep, full = pl.pallas_call(
        functools.partial(block_kernel, rows),
        out_shape=(
            jax.ShapeDtypeStruct((half, width), jnp.bfloat16),
            jax.ShapeDtypeStruct((half, width), jnp.float32),
            jax.ShapeDtypeStruct((half, 2 * width + 4 * units), jnp.bfloat16),
        ),
        in_specs=[VMEM] * 6,
        out_specs=[VMEM] * 3,
        scratch_shapes=[pltpu.VMEM((2 * half, 4 * units), jnp.float32)] + pieces,
        compiler_params=limit,
    )(outer, fourth, gain, *weights)
    peer = lax.ppermute(full, "dp", xor_pairs(count, 1))
    low = jax.ShapeDtypeStruct((2 * half, width + 2 * units), jnp.bfloat16)
    own, away = pl.pallas_call(
        functools.partial(side_kernel, width),
        out_shape=(low, low),
        in_specs=[VMEM] * 2,
        out_specs=[VMEM] * 2,
        compiler_params=pltpu.CompilerParams(vmem_limit_bytes=4 << 20),
    )(full, peer)
    scatter = masks[::-1]
    for step, mask in enumerate(scatter):
        came = lax.ppermute(send, "dp", xor_pairs(count, mask))
        if step + 1 < len(scatter):
            part = keep + came.astype(jnp.float32)
            if step == 0:
                part, nhat, rstd = lax.optimization_barrier((part, nhat, rstd))
            half = part.shape[0] // 2
            send, keep = part[half:].astype(jnp.bfloat16), part[:half]
    far = lax.ppermute(away, "mirror", xor_pairs(mirrors, 1))
    mid = width // 2
    grad_first, grad_second = pl.pallas_call(
        functools.partial(outer_kernel, 8),
        out_shape=(
            jax.ShapeDtypeStruct((mid, units), jnp.bfloat16),
            jax.ShapeDtypeStruct((units, mid), jnp.bfloat16),
        ),
        in_specs=[VMEM] * 2,
        out_specs=[pl.BlockSpec(memory_space=pl.ANY)] * 2,
        scratch_shapes=[
            pltpu.VMEM((2 * far.shape[0], far.shape[1]), jnp.bfloat16),
            pltpu.VMEM((mid, units), jnp.bfloat16),
            pltpu.VMEM((units, mid), jnp.bfloat16),
            pltpu.SemaphoreType.DMA((2, 8)),
        ],
        compiler_params=pltpu.CompilerParams(vmem_limit_bytes=max(6 << 20, 24 * far.size)),
        cost_estimate=pl.CostEstimate(flops=0, bytes_accessed=8 * mid * units, transcendentals=0),
    )(own, far)
    part, grad_first, grad_second = lax.optimization_barrier((part, grad_first, grad_second))
    fwd_out, bwd_out = pl.pallas_call(
        functools.partial(tail_kernel, rows),
        out_shape=(jax.ShapeDtypeStruct((rows, width), jnp.bfloat16),) * 2,
        in_specs=[VMEM] * 6,
        out_specs=[VMEM] * 2,
        compiler_params=pltpu.CompilerParams(vmem_limit_bytes=max(4 << 20, 40 * rows * width * 4)),
    )(part, came, gain, pair, nhat, rstd)
    return (fwd_out[None, None], bwd_out[None, None], grad_first[None], grad_second[None])


def solution(mesh):
    in_specs = (
        P("section", "mirror", "dp", None),
        P("section", "mirror", "dp", None),
        P("section", "mirror", "dp", None),
        P("section", None),
        P("section", None, "dp"),
        P("section", "dp", None),
    )
    out_specs = (
        P("section", "mirror", "dp", None),
        P("section", "mirror", "dp", None),
        P("section", "mirror", "dp"),
        P("section", "dp", "mirror"),
    )
    return jax.shard_map(
        on_device, mesh=mesh, in_specs=in_specs, out_specs=out_specs, check_vma=False
    )
```
